1024 devices in a mesh: gx: 16 (over y, core), gy: 4 (over x), gz: 16 (over z).
Axes of the slice: x: 4, y: 8, z: 16, core: 2. Of those that a mesh axis runs over, the one named last changes fastest.
Arguments:
- old_basis: float32 [4, 128, 64, 2048], P(None, 'gx', 'gy', 'gz'), may hold values from -4 to 4, as said below
- previous: float32 [4, 128, 64, 2048], P(None, 'gx', 'gy', 'gz'), as said below
- incoming: float32 [4, 128, 64, 2048], P(None, 'gx', 'gy', 'gz'), may hold values from -6 to 6
- coefficient: float32 [128, 64, 2048], P('gx', 'gy', 'gz'), may hold values from 0.5 to 4
Outputs:
- orthonormal: float32 [4, 128, 64, 2048], P(None, 'gx', 'gy', 'gz')
- projection: float32 [4, 4], replicated
- triangle: float32 [4, 4], replicated
- preconditioned: float32 [4, 128, 64, 2048], P(None, 'gx', 'gy', 'gz')
- operated: float32 [4, 128, 64, 2048], P(None, 'gx', 'gy', 'gz')
The draws below stay inside these ranges and needn't reach their ends.
Inputs may be any that keep to these rules, and one draw needn't show every extreme that they name: `old_basis`: entries of order one; the basis vectors are independent, so every Gram matrix formed from them is well conditioned. `previous`: entries of order one; each vector has a part outside the span of old_basis of norm of order one under the inner product.
All inputs are finite; a program needn't handle non-finite values.
Results may differ from the reference program's by a relative error of at most 0.0003.
Values sent between devices are 32-bit elements; how exact they have to be, the bound alone decides.
A program may use at most 64 MiB of HBM per device.

```python
import math
import jax
import jax.numpy as jnp
from jax import lax

BLOCK = 4
BASIS = 4
LEVELS = 6
COARSE_SWEEPS = 4
NX = 128
NY = 64
NZ = 2048


def joint_draw(key):
    inner = jax.random.fold_in(key, 4242)
    basis = jax.random.truncated_normal(jax.random.fold_in(inner, 1), -4.0, 4.0, (BASIS, NX, NY, NZ), jnp.float32)
    mixing = jax.random.truncated_normal(jax.random.fold_in(inner, 2), -2.0, 2.0, (BASIS, BLOCK), jnp.float32)
    noise = jax.random.truncated_normal(jax.random.fold_in(inner, 3), -4.0, 4.0, (BLOCK, NX, NY, NZ), jnp.float32)
    ramp_x = 1.0 + 2.0 * jnp.arange(NX, dtype=jnp.float32) / max(NX - 1, 1)
    noise = noise * ramp_x[None, :, None, None]
    combined = jnp.einsum('mj,mxyz->jxyz', mixing, basis) + noise
    return (basis, combined)


def draw_old_basis(key, part):
    return joint_draw(key)[0]


def draw_previous(key, part):
    return joint_draw(key)[1]


def block_levels(own_key, extent, shards, low, top_value):
    def one(position, blocks):
        steps = jax.random.uniform(jax.random.fold_in(jax.random.fold_in(own_key, 6), position), (blocks,), jnp.float32, low / len(shards), top_value / len(shards))
        return jnp.repeat(jnp.exp(steps), extent[position] // blocks).reshape((-1,) + (1,) * (len(extent) - position - 1))

    loudness = one(*shards[0])
    for cut in shards[1:]:
        loudness = loudness * one(*cut)
    return loudness


def bell_draw(own_key, extent, width, reach, split=(), kind=jnp.bfloat16):
    gain = block_levels(own_key, extent, split, -0.22, 0.18) if split else 1.0
    values = jax.random.normal(own_key, extent, jnp.float32) * width * gain
    return jnp.minimum(jnp.maximum(values, -reach), reach).astype(kind)


def setup_inputs(seed: int = 0) -> dict:
    arg_keys = jax.random.split(jax.random.key(seed), 5)
    return {
        "old_basis": draw_old_basis(jax.random.fold_in(arg_keys[4], 71), 0),
        "previous": draw_previous(jax.random.fold_in(arg_keys[4], 71), 0),
        "incoming": bell_draw(arg_keys[2], (BLOCK, NX, NY, NZ), 1.0, 6.0, ((1, 16), (2, 4), (3, 16)), jnp.float32),
        "coefficient": jnp.clip(jnp.exp(math.log(4.0) - 2.0794415 * jax.random.uniform(arg_keys[3], (NX, NY, NZ), jnp.float32) ** block_levels(arg_keys[3], (NX, NY, NZ), ((0, 16), (1, 4), (2, 16)), -0.2, 0.2)), 0.5, 4.0),
    }


OMEGA = 0.8
HIGH = lax.Precision.HIGHEST

def neighbours(field):
    padded = jnp.pad(field, ((0, 0), (1, 1), (1, 1), (1, 1)))
    total = padded[:, 2:, 1:-1, 1:-1] + padded[:, :-2, 1:-1, 1:-1]
    total = total + padded[:, 1:-1, 2:, 1:-1] + padded[:, 1:-1, :-2, 1:-1]
    total = total + padded[:, 1:-1, 1:-1, 2:] + padded[:, 1:-1, 1:-1, :-2]
    return total

def apply_operator(field, coeffs, factor):
    return factor * coeffs * (6.0 * field - neighbours(field))

def restrict(field):
    depth, size_a, size_b, size_c = field.shape
    return field.reshape(depth, size_a // 2, 2, size_b // 2, 2, size_c // 2, 2).mean(axis=(2, 4, 6))

def prolong(field):
    return jnp.repeat(jnp.repeat(jnp.repeat(field, 2, axis=1), 2, axis=2), 2, axis=3)

def vcycle(source, coeff_list, level):
    coeffs = coeff_list[level]
    factor = 0.25 ** level
    diagonal = 6.0 * factor * coeffs
    iterate = OMEGA * source / diagonal
    if level == LEVELS - 1:
        for sweep in range(COARSE_SWEEPS - 1):
            iterate = iterate + OMEGA * (source - apply_operator(iterate, coeffs, factor)) / diagonal
        return iterate
    iterate = iterate + OMEGA * (source - apply_operator(iterate, coeffs, factor)) / diagonal
    residue = source - apply_operator(iterate, coeffs, factor)
    iterate = iterate + prolong(vcycle(restrict(residue), coeff_list, level + 1))
    iterate = iterate + OMEGA * (source - apply_operator(iterate, coeffs, factor)) / diagonal
    return iterate

def triangular_inverse(lower):
    order = lower.shape[0]
    identity = jnp.eye(order, dtype=lower.dtype)
    inverse = jnp.zeros_like(lower)
    for row in range(order):
        values = identity[row] - jnp.dot(lower[row, :row], inverse[:row], precision=HIGH)
        inverse = inverse.at[row].set(values / lower[row, row])
    return inverse

def reference(old_basis, previous, incoming, coefficient):
    total_cells = float(NX * NY * NZ)
    projection = jnp.einsum('mxyz,jxyz->mj', old_basis, previous, precision=HIGH) / total_cells
    remainder = previous - jnp.einsum('mxyz,mj->jxyz', old_basis, projection, precision=HIGH)
    gram = jnp.einsum('ixyz,jxyz->ij', remainder, remainder, precision=HIGH) / total_cells
    lower = jnp.linalg.cholesky(gram)
    inverse = triangular_inverse(lower)
    orthonormal = jnp.einsum('ji,ixyz->jxyz', inverse, remainder, precision=HIGH)
    coeff_list = [coefficient]
    for level in range(LEVELS - 1):
        coeff_list.append(restrict(coeff_list[-1][None])[0])
    preconditioned = vcycle(incoming, coeff_list, 0)
    operated = apply_operator(preconditioned, coefficient, 1.0)
    return (orthonormal, projection, lower.T, preconditioned, operated)
```

```python
import functools

import jax
import jax.numpy as jnp
from jax import lax
from jax.experimental import pallas as pl
from jax.experimental.pallas import tpu as pltpu
from jax.sharding import PartitionSpec as P

OMEGA = 0.8
HIGH = lax.Precision.HIGHEST
MESH = pl.DeviceIdType.MESH
KS = OMEGA / 6.0
F32 = jnp.float32
ANY = pl.ANY

G0, V0, G1, V1, G2, V2, C2, C1, C0 = range(9)


def iota(shape, dim):
    return lax.broadcasted_iota(jnp.int32, shape, dim)


def roll(x, shift, axis):
    n = x.shape[axis]
    shift = shift % n
    return x if shift == 0 else pltpu.roll(x, shift, axis)


def partner_sum(x, axis, s):
    low = (iota(x.shape, axis) & s) == 0
    return x + jnp.where(low, roll(x, x.shape[axis] - s, axis), roll(x, s, axis))


def coarsen(x, s):
    pairs = x.reshape(*x.shape[:-3], x.shape[-3] // 2, 2, *x.shape[-2:])
    x = pairs[..., 0, :, :] + pairs[..., 1, :, :]
    x = partner_sum(x, x.ndim - 2, s)
    return partner_sum(x, x.ndim - 1, s) * 0.125


def kernel(nx, ny, nz, old_hbm, prev_hbm, inc_hbm, coef_hbm,
           ortho_hbm, proj_ref, tri_ref, prec_hbm, oper_hbm,
           old, prev, inc, coef, ortho, oper,
           g0, v0, s0, b1, g1, v1, s1, b2, g2, v2, s2, e2, e1, e0, c1, c2,
           xr, ys, yr, zs, zr, row_s, row_r, plane, zb, gz_s, gz_r,
           cc3, inv3, cc4, inv4, inv5, ebuf,
           in_sem, out_sem, x_send, x_recv, y_send, y_recv, z_send, z_recv,
           ax_send, ax_recv, ay_send, ay_recv, az_send, az_recv, ag_send, ag_recv):
    gx, gy, gz = lax.axis_index("gx"), lax.axis_index("gy"), lax.axis_index("gz")
    X, Y, Z = 8, 16, 128

    def at(dx=0, dy=0, dz=0):
        return (lax.rem(gx + dx + nx, nx), lax.rem(gy + dy + ny, ny), lax.rem(gz + dz + nz, nz))

    loads = [
        pltpu.make_async_copy(src, dst, in_sem.at[i])
        for i, (src, dst) in enumerate(((coef_hbm, coef), (inc_hbm, inc), (old_hbm, old), (prev_hbm, prev)))
    ]
    for load in loads:
        load.start()

    for cond, buf, side in ((gx == 0, xr, 0), (gx == nx - 1, xr, 1), (gy == 0, yr, 0), (gy == ny - 1, yr, 1),
                            (gz == 0, zr, 0), (gz == nz - 1, zr, 1)):
        @pl.when(cond)
        def _():
            buf[side] = jnp.zeros(buf.shape[1:], F32)
    for d in (-2, -1, 1, 2):
        @pl.when((gz + d < 0) | (gz + d >= nz))
        def _():
            zb[:, 2 + d] = jnp.zeros((2,) + zb.shape[2:], F32)

    barrier = pltpu.get_barrier_semaphore()
    for d in range(1, nx):
        pl.semaphore_signal(barrier, inc=1, device_id=at(dx=d), device_id_type=MESH)
    for d in range(1, ny):
        pl.semaphore_signal(barrier, inc=1, device_id=at(dy=d), device_id_type=MESH)
    for d in range(1, nz):
        pl.semaphore_signal(barrier, inc=1, device_id=at(dz=d), device_id_type=MESH)

    ebuf[:, 0] = jnp.zeros(ebuf.shape[:1] + ebuf.shape[2:], F32)
    ebuf[:, ny + 1] = jnp.zeros(ebuf.shape[:1] + ebuf.shape[2:], F32)
    ebuf[:, 1:ny + 1, 0:8] = jnp.zeros((8, ny, 8, Z), F32)
    ebuf[:, 1:ny + 1, 8 + nx:] = jnp.zeros((8, ny, 8, Z), F32)

    lane8, row8 = iota((8, Z), 1), iota((8, Z), 0)
    take_ends = (((row8 == 0) & (lane8 == Z - 1)) | ((row8 == 1) & (lane8 == 0))).astype(F32)

    def faces(e, f, n):
        k = n // 2
        out = []
        for side, d in ((0, 1), (1, -1)):
            def copy(src, dst, ssem, rsem, to):
                return pltpu.make_async_remote_copy(src_ref=src, dst_ref=dst, send_sem=ssem, recv_sem=rsem,
                                                    device_id=to, device_id_type=MESH)
            out.append((copy(zs.at[side, e, pl.ds(0, k)], zr.at[side, e, pl.ds(0, k)], z_send.at[side, e],
                             z_recv.at[side, e], at(dz=d)),
                        (gz + d >= 0) & (gz + d < nz), (gz - d >= 0) & (gz - d < nz)))
            out.append((copy(ys.at[side, e, :, pl.ds(0, n)], yr.at[side, e, :, pl.ds(0, n)], y_send.at[side, e],
                             y_recv.at[side, e], at(dy=d)),
                        (gy + d >= 0) & (gy + d < ny), (gy - d >= 0) & (gy - d < ny)))
            out.append((copy(f.at[:, (n - 1) if side == 0 else 0], xr.at[side, e], x_send.at[side, e],
                             x_recv.at[side, e], at(dx=d)),
                        (gx + d >= 0) & (gx + d < nx), (gx - d >= 0) & (gx - d < nx)))
        return out

    sent = []

    def send(e, f, n):
        k, per = n // 2, 8 // n
        for c in range(k):
            rows = f[c * per:(c + 1) * per].reshape(128, Z)
            ends = lax.dot_general(take_ends, rows, (((1,), (1,)), ((), ())), precision=HIGH,
                                   preferred_element_type=F32)
            zs[0, e, c] = ends[0:1]
            zs[1, e, c] = ends[1:2]
        ys[0, e, :, 0:n] = f[:, :, Y - 1:Y, :]
        ys[1, e, :, 0:n] = f[:, :, 0:1, :]
        for copy, sends, _ in faces(e, f, n):
            sent.append((copy, sends))

            @pl.when(sends)
            def _():
                copy.start()

    def receive(e, f, n):
        for copy, _, receives in faces(e, f, n):
            @pl.when(receives)
            def _():
                copy.wait_recv()

    def along_yz(e, f, n, s, c):
        per = 8 // n
        shape = (per, n, Y, Z)
        x = f[c * per:(c + 1) * per]
        row, lane = iota(shape, 2), iota(shape, 3)
        lo, hi = (yr[side, e, c * per:(c + 1) * per, 0:n] for side in (0, 1))
        total = jnp.where(row >= s, roll(x, s, 2), lo) + jnp.where(row < Y - s, roll(x, Y - s, 2), hi)
        total = total + jnp.where(lane >= s, roll(x, s, 3), 0.0) + jnp.where(lane < Z - s, roll(x, Z - s, 3), 0.0)
        ends = jnp.where(row8 == 0, zr[0, e, c], jnp.where(row8 == 1, zr[1, e, c], 0.0))
        put = (((row8 == 0) & (lane8 < s)) | ((row8 == 1) & (lane8 >= Z - s))).astype(F32)
        halo = lax.dot_general(ends, put, (((0,), (0,)), ((), ())), precision=HIGH, preferred_element_type=F32)
        return x, total + halo.reshape(shape)

    def x_ends(e, n, c):
        per = 8 // n
        return (xr[side, e, c * per:(c + 1) * per][:, None] for side in (0, 1))

    def neighbours(e, f, n, s, c):
        x, total = along_yz(e, f, n, s, c)
        lo, hi = x_ends(e, n, c)
        if n > 1:
            lo = jnp.concatenate([lo, x[:, :-1]], axis=1)
            hi = jnp.concatenate([x[:, 1:], hi], axis=1)
        return x, total + lo + hi

    def second_sweep(e, g, v, n, s):
        receive(e, g, n)
        per = 8 // n
        for c in range(n // 2):
            x, near = neighbours(e, g, n, s, c)
            v[c * per:(c + 1) * per] = 1.2 * x + KS * near

    def residual(e, b, c_hat, g, v, third, n, s, put):
        receive(e, v, n)
        per = 8 // n
        for c in range(n // 2):
            part = slice(c * per, (c + 1) * per)
            x, near = neighbours(e, v, n, s, c)
            third[part] = 0.2 * x + g[part] + KS * near
            put(part, coarsen(b[part] - c_hat * (6.0 * x - near), s))

    def corrected(e, coarse, third, out, n, s):
        receive(e, coarse, n)
        per = 8 // n
        for c in range(n // 2):
            part = slice(c * per, (c + 1) * per)
            x, near = along_yz(e, coarse, n, s, c)
            near = near + x
            lo, hi = x_ends(e, n, c)
            if n > 1:
                lo = jnp.concatenate([lo, x[:, :-1]], axis=1)
                hi = jnp.concatenate([x[:, 1:], hi], axis=1)
            both = jnp.stack([0.2 * x + KS * (near + lo), 0.2 * x + KS * (near + hi)], axis=2)
            out[part] = third[part] + both.reshape(per, 2 * n, Y, Z)

    def line_copies(k):
        return [pltpu.make_async_remote_copy(
            src_ref=row_s.at[k], dst_ref=row_r.at[k, gx], send_sem=ax_send.at[k, d - 1], recv_sem=ax_recv.at[k, d - 1],
            device_id=at(dx=d), device_id_type=MESH) for d in range(1, nx)]

    def plane_copies(k):
        return [pltpu.make_async_remote_copy(
            src_ref=plane.at[k, gy], dst_ref=plane.at[k, gy], send_sem=ay_send.at[k, d - 1],
            recv_sem=ay_recv.at[k, d - 1], device_id=at(dy=d), device_id_type=MESH) for d in range(1, ny)]

    def deep_copies(k):
        return [(pltpu.make_async_remote_copy(
            src_ref=plane.at[k], dst_ref=zb.at[k, 2 - d], send_sem=az_send.at[k, i], recv_sem=az_recv.at[k, i],
            device_id=at(dz=d), device_id_type=MESH), (gz + d >= 0) & (gz + d < nz), (gz - d >= 0) & (gz - d < nz))
            for i, d in enumerate((-2, -1, 1, 2))]

    def start_line(k, row):
        row_s[k] = row
        row_r[k, gx] = row
        for copy in line_copies(k):
            copy.start()

    def start_plane(k):
        for copy in line_copies(k):
            copy.wait()
        plane[k, gy] = row_r[k].reshape(nx, Z)
        for copy in plane_copies(k):
            copy.start()

    def start_deep(k):
        for copy in plane_copies(k):
            copy.wait()
        for copy, sends, _ in deep_copies(k):
            @pl.when(sends)
            def _():
                copy.start()
        zb[k, 2] = plane[k]

    def finish_deep(k):
        for copy, _, receives in deep_copies(k):
            @pl.when(receives)
            def _():
                copy.wait_recv()

    def to_row(blocks):
        q = blocks.shape[0]
        rows = jnp.zeros((8, Z), F32)
        for i in range(q):
            rows = jnp.where(row8 == i, blocks[i], rows)
        pick = (iota((Z, Z), 0) == 8 * (iota((Z, Z), 1) % 16)).astype(F32)
        rows = lax.dot_general(rows, pick, (((1,), (0,)), ((), ())), precision=HIGH, preferred_element_type=F32)
        return jnp.sum(jnp.where(lane8 // 16 == row8, rows, 0.0), axis=0, keepdims=True)

    def spread(k, q):
        shape = (ny, nx, Z)
        group = iota(shape, 2) // 16
        out = jnp.zeros(shape, F32)
        for i in range(5):
            out = jnp.where(group == i, roll(zb[k, i], 16 * (i - q), 2), out)
        return out

    loads[0].wait()
    loads[1].wait()
    c_fine = coef[...]
    scale = KS / c_fine
    for v in range(4):
        g0[v] = inc[v] * scale
    c1[...] = coarsen(c_fine, 1)
    c2[...] = coarsen(c1[...], 2)
    c3 = coarsen(c2[...], 4)

    total_devices = (nx - 1) + (ny - 1) + (nz - 1)
    pl.semaphore_wait(barrier, total_devices)
    send(G0, g0, 8)

    loads[2].wait()
    loads[3].wait()
    pairs = [("p", m, j) for m in range(4) for j in range(4)]
    pairs += [("s", i, j) for i in range(4) for j in range(i, 4)]
    pairs += [("c", i, j) for i in range(4) for j in range(i, 4)]
    sums = [None] * len(pairs)
    for x in range(X):
        vo = [old[m, x] for m in range(4)]
        vp = [prev[m, x] for m in range(4)]
        for p, (kind, i, j) in enumerate(pairs):
            a = (vp if kind == "s" else vo)[i]
            b = (vo if kind == "c" else vp)[j]
            ab = a * b
            ab = ab[0:8] + ab[8:16]
            sums[p] = ab if sums[p] is None else sums[p] + ab
    rows = [jnp.sum(a, axis=0, keepdims=True) for a in sums] + [jnp.zeros((4, Z), F32)]
    rows = jnp.sum(jnp.concatenate(rows, axis=0), axis=1, keepdims=True)
    at_lane = iota((40, Z), 1) == iota((40, Z), 0) + 64
    gram_row = jnp.sum(jnp.where(at_lane, rows, 0.0), axis=0, keepdims=True)
    start_line(0, to_row(c3.reshape(2, 8, Z)) + gram_row)

    second_sweep(G0, g0, v0, 8, 1)
    send(V0, v0, 8)
    start_plane(0)

    def put_b1(part, r):
        b1[part] = r
        g1[part] = r * scale1
    scale1 = (4.0 * KS) / c1[...]
    residual(V0, inc, c_fine, g0, v0, s0, 8, 1, put_b1)
    send(G1, g1, 4)
    start_deep(0)
    gram_line = jnp.sum(plane[0].reshape(ny * nx, Z), axis=0, keepdims=True)
    gz_s[...] = gram_line
    gz_r[gz] = gram_line
    gram_copies = [pltpu.make_async_remote_copy(
        src_ref=gz_s, dst_ref=gz_r.at[gz], send_sem=ag_send.at[d - 1], recv_sem=ag_recv.at[d - 1],
        device_id=at(dz=d), device_id_type=MESH) for d in range(1, nz)]
    for copy in gram_copies:
        copy.start()

    second_sweep(G1, g1, v1, 4, 2)
    send(V1, v1, 4)
    scale2 = (16.0 * KS) / c2[...]

    def put_b2(part, r):
        b2[part] = r
        g2[part] = r * scale2
    residual(V1, b1, 0.25 * c1[...], g1, v1, s1, 4, 2, put_b2)
    send(G2, g2, 2)
    second_sweep(G2, g2, v2, 2, 4)
    send(V2, v2, 2)
    held = []
    residual(V2, b2, 0.0625 * c2[...], g2, v2, s2, 2, 4, lambda part, r: held.append(r))
    start_line(1, to_row(held[0].reshape(8, 8, Z)))

    shape = (ny, nx, Z)
    lanes = iota(shape, 2)
    place = (gz - 2) * 16 + lanes
    inside = (place >= 0) & (place < nz * 16) & (lanes < 80)
    km = jnp.where(inside, KS, 0.0)
    finish_deep(0)
    c3g = [jnp.where(inside, spread(0, q), 1.0) for q in range(2)]
    for q in range(2):
        cc3[q] = (1.0 / 64) * c3g[q]
        inv3[q] = jnp.where(inside, (64.0 * KS) / c3g[q], 0.0)

    def coarsen_gathered(x, s):
        x = partner_sum(x, 1, s)
        return partner_sum(x, 2, s) * 0.125
    c4g = coarsen_gathered(c3g[0] + c3g[1], 1)
    cc4[...] = (1.0 / 256) * c4g
    inv4[...] = jnp.where(inside, (256.0 * KS) / c4g, 0.0)
    halved = c4g.reshape(ny // 2, 2, nx, Z)
    c5g = coarsen_gathered(halved[:, 0] + halved[:, 1], 2)
    inv5[...] = jnp.where(inside[:ny // 2], (1024.0 * KS) / c5g, 0.0)

    start_plane(1)

    for copy in gram_copies:
        copy.wait()
    line = jnp.sum(gz_r[...].reshape(nz, Z), axis=0, keepdims=True)
    column = jnp.sum(jnp.where(at_lane, line, 0.0), axis=1, keepdims=True)
    column = column * (1.0 / float(nx * ny * nz * X * Y * Z))
    value = {key: column[p:p + 1] for p, key in enumerate(pairs)}
    for kind in "sc":
        for i in range(4):
            for j in range(i):
                value[kind, i, j] = value[kind, j, i]
    proj = [[value["p", m, j] for j in range(4)] for m in range(4)]
    mixed = [[sum(value["c", m, n] * proj[n][j] for n in range(4)) for j in range(4)] for m in range(4)]
    low = [[None] * 4 for _ in range(4)]
    inverse = [[None] * 4 for _ in range(4)]
    for j in range(4):
        for i in range(j, 4):
            g = value["s", i, j] + sum(proj[m][i] * (mixed[m][j] - 2.0 * proj[m][j]) for m in range(4))
            for k in range(j):
                g = g - low[i][k] * low[j][k]
            low[i][j] = jnp.sqrt(g) if i == j else g / low[j][j]
    for j in range(4):
        inverse[j][j] = 1.0 / low[j][j]
        for i in range(j + 1, 4):
            inverse[i][j] = -sum(low[i][k] * inverse[k][j] for k in range(j, i)) * (1.0 / low[i][i])
    r4, l4 = iota((4, 4), 0), iota((4, 4), 1)
    out_p, out_t = jnp.zeros((4, 4), F32), jnp.zeros((4, 4), F32)
    for i in range(4):
        for j in range(4):
            here = (r4 == i) & (l4 == j)
            out_p = jnp.where(here, proj[i][j], out_p)
            if j >= i:
                out_t = jnp.where(here, low[j][i], out_t)
    proj_ref[...] = out_p
    tri_ref[...] = out_t
    wide = lambda a: jnp.broadcast_to(a, (8, Z))
    proj_w = [[wide(a) for a in line_] for line_ in proj]
    inv_w = [[wide(inverse[j][i]) if i <= j else None for i in range(4)] for j in range(4)]
    for x in range(X):
        for h in range(2):
            part = slice(8 * h, 8 * h + 8)
            vo = [old[m, x, part] for m in range(4)]
            rem = [prev[j, x, part] - sum(proj_w[m][j] * vo[m] for m in range(4)) for j in range(4)]
            for j in range(4):
                ortho[j, x, part] = sum(inv_w[j][i] * rem[i] for i in range(j + 1))
    outs = [pltpu.make_async_copy(ortho, ortho_hbm, out_sem.at[0])]
    outs[0].start()

    start_deep(1)
    finish_deep(1)

    rows_i = iota(shape, 1)
    zero = jnp.zeros((1, nx, Z), F32)

    def along_xz(v, s):
        r = rows_i[:v.shape[0]]
        out = jnp.where(r >= s, roll(v, s, 1), 0.0) + jnp.where(r < nx - s, roll(v, nx - s, 1), 0.0)
        return out + roll(v, s, 2) + roll(v, Z - s, 2)

    def up(v):
        return zero if v.shape[0] == 1 else jnp.concatenate([v[1:], zero], axis=0)

    def down(v):
        return zero if v.shape[0] == 1 else jnp.concatenate([zero, v[:-1]], axis=0)

    def near3(v):
        return [along_xz(v[0], 1) + v[1] + down(v[1]), along_xz(v[1], 1) + v[0] + up(v[0])]

    def near_coarse(v, s):
        return along_xz(v, s) + up(v) + down(v)

    km5 = km[:ny // 2]
    for vec in range(4):
        b = [spread(1, 2 * vec + q) for q in range(2)]
        g = [b[q] * inv3[q] for q in range(2)]
        near = near3(g)
        v = [1.2 * g[q] + km * near[q] for q in range(2)]
        near = near3(v)
        third = [0.2 * v[q] + g[q] + km * near[q] for q in range(2)]
        r = [b[q] - cc3[q] * (6.0 * v[q] - near[q]) for q in range(2)]
        b4 = coarsen_gathered(jnp.where(inside, r[0] + r[1], 0.0), 1)
        g4 = b4 * inv4[...]
        v4 = 1.2 * g4 + km * near_coarse(g4, 2)
        n4 = near_coarse(v4, 2)
        third4 = 0.2 * v4 + g4 + km * n4
        r4_ = b4 - cc4[...] * (6.0 * v4 - n4)
        r4_ = jnp.where(inside, r4_, 0.0).reshape(ny // 2, 2, nx, Z)
        g5 = coarsen_gathered(r4_[:, 0] + r4_[:, 1], 2) * inv5[...]
        v5 = g5
        for _ in range(3):
            v5 = 0.2 * v5 + g5 + km5 * near_coarse(v5, 4)
        p4 = jnp.stack([v5, v5], axis=1).reshape(ny, nx, Z)
        e4 = third4 + 0.2 * p4 + km * near_coarse(p4, 2)
        xz = along_xz(e4, 1) + 1.2 / 6.0 * 0.0
        ebuf[2 * vec, 1:ny + 1, 8:8 + nx] = third[0] + 0.2 * e4 + km * (xz + e4 + down(e4))
        ebuf[2 * vec + 1, 1:ny + 1, 8:8 + nx] = third[1] + 0.2 * e4 + km * (xz + e4 + up(e4))

    def cells(dy, dx):
        return ebuf[:, gy + 1 + dy, pl.ds(8 + gx + dx, 1), :].reshape(8, Z)
    li, lj = iota((Z, Z), 0), iota((Z, Z), 1)
    widen = (li == 32 + lj // 8).astype(F32)
    beside = ((li == 31 + (lj + 4) // 8) | (li == 32 + (lj + 4) // 8)).astype(F32)
    own = cells(0, 0)
    stacked = jnp.concatenate([own, cells(0, -1), cells(0, 1), cells(-1, 0), cells(1, 0)], axis=0)
    wide_rows = lax.dot_general(stacked, widen, (((1,), (0,)), ((), ())), precision=HIGH, preferred_element_type=F32)
    z_rows = lax.dot_general(own, beside, (((1,), (0,)), ((), ())), precision=HIGH, preferred_element_type=F32)
    for vec in range(4):
        q = [2 * vec, 2 * vec + 1]
        a = [wide(wide_rows[i:i + 1]) for i in q]
        x_lo = [wide(wide_rows[8 + i:9 + i]) for i in q]
        x_hi = [wide(wide_rows[16 + i:17 + i]) for i in q]
        y_lo = wide(wide_rows[24 + q[1]:25 + q[1]])
        y_hi = wide(wide_rows[32 + q[0]:33 + q[0]])
        z_sum = [wide(z_rows[i:i + 1]) for i in q]
        mid = a[0] + a[1]
        y_sum = [jnp.where(row8 < 4, y_lo + a[0], mid), jnp.where(row8 < 4, mid, a[1] + y_hi)]
        for h in range(2):
            part = slice(8 * h, 8 * h + 8)
            base = 0.2 * a[h] + KS * (y_sum[h] + z_sum[h] + a[h])
            e2[vec, 0, part] = s2[vec, 0, part] + base + KS * x_lo[h]
            e2[vec, 1, part] = s2[vec, 1, part] + base + KS * x_hi[h]

    send(C2, e2, 2)
    corrected(C2, e2, s1, e1, 2, 2)
    send(C1, e1, 4)
    corrected(C1, e1, s0, e0, 4, 1)
    send(C0, e0, 8)
    outs.append(pltpu.make_async_copy(e0, prec_hbm, out_sem.at[1]))
    outs[1].start()
    receive(C0, e0, 8)
    for c in range(4):
        x, near = neighbours(C0, e0, 8, 1, c)
        oper[c:c + 1] = c_fine * (6.0 * x - near)
    outs.append(pltpu.make_async_copy(oper, oper_hbm, out_sem.at[2]))
    outs[2].start()
    for copy, sends in sent:
        @pl.when(sends)
        def _():
            copy.wait_send()
    for k in range(2):
        for copy, sends, _ in deep_copies(k):
            @pl.when(sends)
            def _():
                copy.wait_send()
    for out in outs:
        out.wait()


def per_device(shape, old_basis, previous, incoming, coefficient):
    nx, ny, nz = shape
    big = pltpu.VMEM((4, 8, 16, 128), F32)
    mid = pltpu.VMEM((4, 4, 16, 128), F32)
    low = pltpu.VMEM((4, 2, 16, 128), F32)
    dma = pltpu.SemaphoreType.DMA
    vm = lambda *s: pltpu.VMEM(s, F32)
    whole = jax.ShapeDtypeStruct((4, 8, 16, 128), F32)
    small = jax.ShapeDtypeStruct((4, 4), F32)
    any_spec = pl.BlockSpec(memory_space=pl.ANY)
    vmem_spec = pl.BlockSpec(memory_space=pltpu.VMEM)
    return pl.pallas_call(
        functools.partial(kernel, nx, ny, nz),
        out_shape=(whole, small, small, whole, whole),
        in_specs=[any_spec] * 4,
        out_specs=(any_spec, vmem_spec, vmem_spec, any_spec, any_spec),
        scratch_shapes=[
            big, big, big, vm(8, 16, 128), big, big,
            big, big, big, mid, mid, mid, mid, low, low, low, low, low, mid, big, vm(4, 16, 128), vm(2, 16, 128),
            vm(2, 9, 4, 16, 128), vm(2, 9, 4, 8, 1, 128), vm(2, 9, 4, 8, 1, 128),
            vm(2, 9, 4, 1, 128), vm(2, 9, 4, 1, 128),
            vm(2, 1, 128), vm(2, nx, 1, 128), vm(2, ny, nx, 128), vm(2, 5, ny, nx, 128), vm(1, 128), vm(nz, 1, 128),
            vm(2, ny, nx, 128), vm(2, ny, nx, 128), vm(ny, nx, 128), vm(ny, nx, 128), vm(ny // 2, nx, 128),
            vm(8, ny + 2, nx + 16, 128),
            dma((4,)), dma((3,)), dma((2, 9)), dma((2, 9)), dma((2, 9)), dma((2, 9)), dma((2, 9)), dma((2, 9)),
            dma((2, nx - 1)), dma((2, nx - 1)), dma((2, ny - 1)), dma((2, ny - 1)), dma((2, 4)), dma((2, 4)),
            dma((nz - 1,)), dma((nz - 1,)),
        ],
        compiler_params=pltpu.CompilerParams(collective_id=0, has_side_effects=True),
    )(old_basis, previous, incoming, coefficient)


def solution(mesh):
    shape = (mesh.shape["gx"], mesh.shape["gy"], mesh.shape["gz"])
    split = P(None, "gx", "gy", "gz")
    return jax.shard_map(
        functools.partial(per_device, shape), mesh=mesh,
        in_specs=(split, split, split, P("gx", "gy", "gz")),
        out_specs=(split, P(), P(), split, split), check_vma=False,
    )
```

```python
import functools

import jax
import jax.numpy as jnp
from jax import lax
from jax.experimental import pallas as pl
from jax.experimental.pallas import tpu as pltpu
from jax.sharding import PartitionSpec as P

OMEGA = 0.8
HIGH = lax.Precision.HIGHEST
MESH = pl.DeviceIdType.MESH
KS = OMEGA / 6.0
F32 = jnp.float32
ANY = pl.ANY

G0, V0, G1, V1, G2, V2, T2, C1, C0, C2 = range(10)


def iota(shape, dim):
    return lax.broadcasted_iota(jnp.int32, shape, dim)


def roll(x, shift, axis):
    n = x.shape[axis]
    shift = shift % n
    return x if shift == 0 else pltpu.roll(x, shift, axis)


def partner_sum(x, axis, s):
    low = (iota(x.shape, axis) & s) == 0
    return x + jnp.where(low, roll(x, x.shape[axis] - s, axis), roll(x, s, axis))


def coarsen(x, s):
    pairs = x.reshape(*x.shape[:-3], x.shape[-3] // 2, 2, *x.shape[-2:])
    x = pairs[..., 0, :, :] + pairs[..., 1, :, :]
    x = partner_sum(x, x.ndim - 2, s)
    return partner_sum(x, x.ndim - 1, s) * 0.125


def kernel(nx, ny, nz, old_hbm, prev_hbm, inc_hbm, coef_hbm,
           ortho, proj_ref, tri_ref, e0, oper,
           old, prev, inc, coef,
           g0, v0, s0, b1, g1, v1, s1, b2, g2, v2, s2, e2, e1, c1, c2, beyond,
           xs, xc, xr, ys, yr, zs, zr, row_s, row_r, line_b, zb, gz_s, gz_r,
           cc3, inv3, cc4, inv4, inv5, ebuf,
           in_sem, x_send, x_recv, y_send, y_recv, z_send, z_recv,
           ax_send, ax_recv, az_send, az_recv, ag_send, ag_recv):
    gx, gy, gz = lax.axis_index("gx"), lax.axis_index("gy"), lax.axis_index("gz")
    X, Y, Z = 8, 16, 128

    def at(dx=0, dy=0, dz=0):
        return (lax.rem(gx + dx + nx, nx), lax.rem(gy + dy + ny, ny), lax.rem(gz + dz + nz, nz))

    loads = [
        pltpu.make_async_copy(src, dst, in_sem.at[i])
        for i, (src, dst) in enumerate(((coef_hbm, coef), (inc_hbm, inc), (old_hbm, old), (prev_hbm, prev)))
    ]
    for load in loads:
        load.start()

    for cond, buf, side in ((gx == 0, xr, 0), (gx == nx - 1, xr, 1), (gx == 0, xc, 0), (gx == nx - 1, xc, 1), (gy == 0, yr, 0), (gy == ny - 1, yr, 1),
                            (gz == 0, zr, 0), (gz == nz - 1, zr, 1)):
        @pl.when(cond)
        def _():
            buf[side] = jnp.zeros(buf.shape[1:], F32)
    for d in (-2, -1, 1, 2):
        @pl.when((gz + d < 0) | (gz + d >= nz))
        def _():
            zb[:, 2 + d] = jnp.zeros((2,) + zb.shape[2:], F32)

    barrier = pltpu.get_barrier_semaphore()
    for d in range(1, nx):
        pl.semaphore_signal(barrier, inc=1, device_id=at(dx=d), device_id_type=MESH)
    for d in range(1, nz):
        pl.semaphore_signal(barrier, inc=1, device_id=at(dz=d), device_id_type=MESH)
    partners = jnp.int32(nx - 1 + nz - 1)
    for dz in range(-2, 3):
        reach = (gz + dz >= 0) & (gz + dz < nz)
        partners = partners + jnp.where(reach, ny - 1, 0)

        @pl.when(reach)
        def _():
            for dy in range(1, ny):
                pl.semaphore_signal(barrier, inc=1, device_id=at(dy=dy, dz=dz), device_id_type=MESH)

    ebuf[:, 0] = jnp.zeros(ebuf.shape[:1] + ebuf.shape[2:], F32)
    ebuf[:, ny + 1] = jnp.zeros(ebuf.shape[:1] + ebuf.shape[2:], F32)
    ebuf[:, 1:ny + 1, 0:8] = jnp.zeros((8, ny, 8, Z), F32)
    ebuf[:, 1:ny + 1, 8 + nx:] = jnp.zeros((8, ny, 8, Z), F32)

    lane8, row8 = iota((8, Z), 1), iota((8, Z), 0)
    take_ends = (((row8 == 0) & (lane8 == Z - 1)) | ((row8 == 1) & (lane8 == 0))).astype(F32)

    def copy_to(src, dst, ssem, rsem, to):
        return pltpu.make_async_remote_copy(src_ref=src, dst_ref=dst, send_sem=ssem, recv_sem=rsem, device_id=to,
                                            device_id_type=MESH)

    def faces(e, f, n, axis):
        k = n // 2
        out = []
        for side, d in ((0, 1), (1, -1)):
            if axis == 0:
                if n == 8:
                    src, dst = f.at[:, (n - 1) if side == 0 else 0], xr.at[side, e]
                else:
                    src, dst = xs.at[side, e, pl.ds(0, n)], xc.at[side, e, pl.ds(0, n)]
                copy = copy_to(src, dst, x_send.at[side, e], x_recv.at[side, e], at(dx=d))
                place, count = gx, nx
            elif axis == 1:
                copy = copy_to(ys.at[side, e, :, pl.ds(0, n)], yr.at[side, e, :, pl.ds(0, n)], y_send.at[side, e],
                               y_recv.at[side, e], at(dy=d))
                place, count = gy, ny
            else:
                copy = copy_to(zs.at[side, e, pl.ds(0, k)], zr.at[side, e, pl.ds(0, k)], z_send.at[side, e],
                               z_recv.at[side, e], at(dz=d))
                place, count = gz, nz
            out.append((copy, (place + d >= 0) & (place + d < count), (place - d >= 0) & (place - d < count)))
        return out

    sent = []

    def start(e, f, n, axis):
        for copy, sends, _ in faces(e, f, n, axis):
            sent.append((copy, sends))

            @pl.when(sends)
            def _():
                copy.start()

    def send(e, f, n):
        k, per = n // 2, 8 // n
        for side, x in ((0, n - 1), (1, 0)):
            for v in range(4):
                if n == 4:
                    xs[side, e, v] = f[v, x, pl.ds(0, 8, stride=2), :]
                elif n == 2:
                    xs[side, e, v // 2, 4 * (v % 2):4 * (v % 2) + 4] = f[v, x, pl.ds(0, 4, stride=4), :]
        start(e, f, n, 0)
        ys[0, e, :, 0:n] = f[:, :, Y - 1:Y, :]
        ys[1, e, :, 0:n] = f[:, :, 0:1, :]
        start(e, f, n, 1)
        for c in range(k):
            rows = f[c * per:(c + 1) * per].reshape(128, Z)
            ends = lax.dot_general(take_ends, rows, (((1,), (1,)), ((), ())), precision=HIGH,
                                   preferred_element_type=F32)
            zs[0, e, c] = ends[0:1]
            zs[1, e, c] = ends[1:2]
        start(e, f, n, 2)

    def receive(e, f, n):
        for axis in range(3):
            for copy, _, receives in faces(e, f, n, axis):
                @pl.when(receives)
                def _():
                    copy.wait_recv()
        if n < 8:
            for side in range(2):
                for v in range(4):
                    if n == 4:
                        half = xc[side, e, v]
                        for i in range(2):
                            xr[side, e, v, pl.ds(i, 8, stride=2), :] = half
                    else:
                        half = xc[side, e, v // 2, 4 * (v % 2):4 * (v % 2) + 4]
                        for i in range(4):
                            xr[side, e, v, pl.ds(i, 4, stride=4), :] = half

    def along_yz(e, f, n, s, c):
        per = 8 // n
        shape = (per, n, Y, Z)
        x = f[c * per:(c + 1) * per]
        row, lane = iota(shape, 2), iota(shape, 3)
        lo, hi = (yr[side, e, c * per:(c + 1) * per, 0:n] for side in (0, 1))
        total = jnp.where(row >= s, roll(x, s, 2), lo) + jnp.where(row < Y - s, roll(x, Y - s, 2), hi)
        if e == C2:
            out = beyond[c * per:(c + 1) * per]
            return x, (total + jnp.where(lane >= s, roll(x, s, 3), roll(out, s, 3))
                       + jnp.where(lane < Z - s, roll(x, Z - s, 3), roll(out, Z - s, 3)))
        total = total + jnp.where(lane >= s, roll(x, s, 3), 0.0) + jnp.where(lane < Z - s, roll(x, Z - s, 3), 0.0)
        ends = jnp.where(row8 == 0, zr[0, e, c], jnp.where(row8 == 1, zr[1, e, c], 0.0))
        put = (((row8 == 0) & (lane8 < s)) | ((row8 == 1) & (lane8 >= Z - s))).astype(F32)
        halo = lax.dot_general(ends, put, (((0,), (0,)), ((), ())), precision=HIGH, preferred_element_type=F32)
        return x, total + halo.reshape(shape)

    def x_ends(e, n, c):
        per = 8 // n
        return (xr[side, e, c * per:(c + 1) * per][:, None] for side in (0, 1))

    def neighbours(e, f, n, s, c):
        x, total = along_yz(e, f, n, s, c)
        lo, hi = x_ends(e, n, c)
        if n > 1:
            lo = jnp.concatenate([lo, x[:, :-1]], axis=1)
            hi = jnp.concatenate([x[:, 1:], hi], axis=1)
        return x, total + lo + hi

    def second_sweep(e, g, v, n, s):
        receive(e, g, n)
        per = 8 // n
        for c in range(n // 2):
            x, near = neighbours(e, g, n, s, c)
            v[c * per:(c + 1) * per] = 1.2 * x + KS * near

    def residual(e, b, c_hat, g, v, third, n, s, put):
        receive(e, v, n)
        per = 8 // n
        for c in range(n // 2):
            part = slice(c * per, (c + 1) * per)
            x, near = neighbours(e, v, n, s, c)
            third[part] = 0.2 * x + g[part] + KS * near
            put(part, coarsen(b[part] - c_hat * (6.0 * x - near), s))

    def corrected(e, coarse, third, out, n, s):
        per = 8 // n
        for c in range(n // 2):
            part = slice(c * per, (c + 1) * per)
            x, near = along_yz(e, coarse, n, s, c)
            near = near + x
            lo, hi = x_ends(e, n, c)
            if n > 1:
                lo = jnp.concatenate([lo, x[:, :-1]], axis=1)
                hi = jnp.concatenate([x[:, 1:], hi], axis=1)
            both = jnp.stack([0.2 * x + KS * (near + lo), 0.2 * x + KS * (near + hi)], axis=2)
            out[part] = third[part] + both.reshape(per, 2 * n, Y, Z)

    def line_copies(k):
        return [pltpu.make_async_remote_copy(
            src_ref=row_s.at[k], dst_ref=row_r.at[k, gx], send_sem=ax_send.at[k, d - 1], recv_sem=ax_recv.at[k, d - 1],
            device_id=at(dx=d), device_id_type=MESH) for d in range(1, nx)]

    slabs = [(dy, dz) for dz in (0, -1, 1, -2, 2) for dy in range(ny) if dy or dz]

    def deep_copies(k):
        return [(copy_to(line_b.at[k], zb.at[k, 2 - dz, gy], az_send.at[k, i], az_recv.at[k, i], at(dy=dy, dz=dz)),
                 (gz + dz >= 0) & (gz + dz < nz), (gz - dz >= 0) & (gz - dz < nz)) for i, (dy, dz) in enumerate(slabs)]

    def start_line(k, row):
        row_s[k] = row
        row_r[k, gx] = row
        for copy in line_copies(k):
            copy.start()

    def start_deep(k):
        for copy in line_copies(k):
            copy.wait()
        line_b[k] = row_r[k].reshape(nx, Z)
        for copy, sends, _ in deep_copies(k):
            @pl.when(sends)
            def _():
                copy.start()
        zb[k, 2, gy] = line_b[k]

    def finish_deep(k):
        for copy, _, receives in deep_copies(k):
            @pl.when(receives)
            def _():
                copy.wait_recv()

    def to_row(blocks):
        q = blocks.shape[0]
        rows = jnp.zeros((8, Z), F32)
        for i in range(q):
            rows = jnp.where(row8 == i, blocks[i], rows)
        pick = (iota((Z, Z), 0) == 8 * (iota((Z, Z), 1) % 16)).astype(F32)
        rows = lax.dot_general(rows, pick, (((1,), (0,)), ((), ())), precision=HIGH, preferred_element_type=F32)
        return jnp.sum(jnp.where(lane8 // 16 == row8, rows, 0.0), axis=0, keepdims=True)

    def spread(k, q):
        shape = (ny, nx, Z)
        group = iota(shape, 2) // 16
        out = jnp.zeros(shape, F32)
        for i in range(5):
            out = jnp.where(group == i, roll(zb[k, i], 16 * (i - q), 2), out)
        return out

    loads[0].wait()
    loads[1].wait()
    c_fine = coef[...]
    scale = KS / c_fine
    for v in range(4):
        g0[v] = inc[v] * scale
    c1[...] = coarsen(c_fine, 1)
    c2[...] = coarsen(c1[...], 2)
    c3 = coarsen(c2[...], 4)

    pl.semaphore_wait(barrier, partners)
    send(G0, g0, 8)

    loads[2].wait()
    loads[3].wait()
    pairs = [("p", m, j) for m in range(4) for j in range(4)]
    pairs += [("s", i, j) for i in range(4) for j in range(i, 4)]
    pairs += [("c", i, j) for i in range(4) for j in range(i, 4)]
    sums = [None] * len(pairs)
    for x in range(X):
        vo = [old[m, x] for m in range(4)]
        vp = [prev[m, x] for m in range(4)]
        for p, (kind, i, j) in enumerate(pairs):
            a = (vp if kind == "s" else vo)[i]
            b = (vo if kind == "c" else vp)[j]
            ab = a * b
            ab = ab[0:8] + ab[8:16]
            sums[p] = ab if sums[p] is None else sums[p] + ab
    rows = [jnp.sum(a, axis=0, keepdims=True) for a in sums] + [jnp.zeros((4, Z), F32)]
    rows = jnp.sum(jnp.concatenate(rows, axis=0), axis=1, keepdims=True)
    at_lane = iota((40, Z), 1) == iota((40, Z), 0) + 64
    gram_row = jnp.sum(jnp.where(at_lane, rows, 0.0), axis=0, keepdims=True)
    start_line(0, to_row(c3.reshape(2, 8, Z)) + gram_row)

    second_sweep(G0, g0, v0, 8, 1)
    send(V0, v0, 8)
    start_deep(0)

    def put_b1(part, r):
        b1[part] = r
        g1[part] = r * scale1
    scale1 = (4.0 * KS) / c1[...]
    residual(V0, inc, c_fine, g0, v0, s0, 8, 1, put_b1)
    send(G1, g1, 4)
    finish_deep(0)
    gram_line = jnp.sum(zb[0, 2].reshape(ny * nx, Z), axis=0, keepdims=True)
    gz_s[...] = gram_line
    gz_r[gz] = gram_line
    gram_copies = [pltpu.make_async_remote_copy(
        src_ref=gz_s, dst_ref=gz_r.at[gz], send_sem=ag_send.at[d - 1], recv_sem=ag_recv.at[d - 1],
        device_id=at(dz=d), device_id_type=MESH) for d in range(1, nz)]
    for copy in gram_copies:
        copy.start()

    second_sweep(G1, g1, v1, 4, 2)
    send(V1, v1, 4)
    scale2 = (16.0 * KS) / c2[...]

    def put_b2(part, r):
        b2[part] = r
        g2[part] = r * scale2
    residual(V1, b1, 0.25 * c1[...], g1, v1, s1, 4, 2, put_b2)
    send(G2, g2, 2)
    second_sweep(G2, g2, v2, 2, 4)
    send(V2, v2, 2)
    held = []
    residual(V2, b2, 0.0625 * c2[...], g2, v2, s2, 2, 4, lambda part, r: held.append(r))
    start_line(1, to_row(held[0].reshape(8, 8, Z)))
    send(T2, s2, 2)

    shape = (ny, nx, Z)
    lanes = iota(shape, 2)
    place = (gz - 2) * 16 + lanes
    inside = (place >= 0) & (place < nz * 16) & (lanes < 80)
    km = jnp.where(inside, KS, 0.0)
    c3g = [jnp.where(inside, spread(0, q), 1.0) for q in range(2)]
    for q in range(2):
        cc3[q] = (1.0 / 64) * c3g[q]
        inv3[q] = jnp.where(inside, (64.0 * KS) / c3g[q], 0.0)

    def coarsen_gathered(x, s):
        x = partner_sum(x, 1, s)
        return partner_sum(x, 2, s) * 0.125
    c4g = coarsen_gathered(c3g[0] + c3g[1], 1)
    cc4[...] = (1.0 / 256) * c4g
    inv4[...] = jnp.where(inside, (256.0 * KS) / c4g, 0.0)
    halved = c4g.reshape(ny // 2, 2, nx, Z)
    c5g = coarsen_gathered(halved[:, 0] + halved[:, 1], 2)
    inv5[...] = jnp.where(inside[:ny // 2], (1024.0 * KS) / c5g, 0.0)

    start_deep(1)

    for copy in gram_copies:
        copy.wait()
    line = jnp.sum(gz_r[...].reshape(nz, Z), axis=0, keepdims=True)
    column = jnp.sum(jnp.where(at_lane, line, 0.0), axis=1, keepdims=True)
    column = column * (1.0 / float(nx * ny * nz * X * Y * Z))
    value = {key: column[p:p + 1] for p, key in enumerate(pairs)}
    for kind in "sc":
        for i in range(4):
            for j in range(i):
                value[kind, i, j] = value[kind, j, i]
    proj = [[value["p", m, j] for j in range(4)] for m in range(4)]
    mixed = [[sum(value["c", m, n] * proj[n][j] for n in range(4)) for j in range(4)] for m in range(4)]
    low = [[None] * 4 for _ in range(4)]
    inverse = [[None] * 4 for _ in range(4)]
    for j in range(4):
        for i in range(j, 4):
            g = value["s", i, j] + sum(proj[m][i] * (mixed[m][j] - 2.0 * proj[m][j]) for m in range(4))
            for k in range(j):
                g = g - low[i][k] * low[j][k]
            low[i][j] = jnp.sqrt(g) if i == j else g / low[j][j]
    for j in range(4):
        inverse[j][j] = 1.0 / low[j][j]
        for i in range(j + 1, 4):
            inverse[i][j] = -sum(low[i][k] * inverse[k][j] for k in range(j, i)) * (1.0 / low[i][i])
    r4, l4 = iota((4, 4), 0), iota((4, 4), 1)
    out_p, out_t = jnp.zeros((4, 4), F32), jnp.zeros((4, 4), F32)
    for i in range(4):
        for j in range(4):
            here = (r4 == i) & (l4 == j)
            out_p = jnp.where(here, proj[i][j], out_p)
            if j >= i:
                out_t = jnp.where(here, low[j][i], out_t)
    proj_ref[...] = out_p
    tri_ref[...] = out_t
    wide = lambda a: jnp.broadcast_to(a, (8, Z))
    proj_w = [[wide(a) for a in line_] for line_ in proj]
    inv_w = [[wide(inverse[j][i]) if i <= j else None for i in range(4)] for j in range(4)]
    for x in range(X):
        for h in range(2):
            part = slice(8 * h, 8 * h + 8)
            vo = [old[m, x, part] for m in range(4)]
            rem = [prev[j, x, part] - sum(proj_w[m][j] * vo[m] for m in range(4)) for j in range(4)]
            for j in range(4):
                ortho[j, x, part] = sum(inv_w[j][i] * rem[i] for i in range(j + 1))

    finish_deep(1)

    rows_i = iota(shape, 1)
    zero = jnp.zeros((1, nx, Z), F32)

    def along_xz(v, s):
        r = rows_i[:v.shape[0]]
        out = jnp.where(r >= s, roll(v, s, 1), 0.0) + jnp.where(r < nx - s, roll(v, nx - s, 1), 0.0)
        return out + roll(v, s, 2) + roll(v, Z - s, 2)

    def up(v):
        return zero if v.shape[0] == 1 else jnp.concatenate([v[1:], zero], axis=0)

    def down(v):
        return zero if v.shape[0] == 1 else jnp.concatenate([zero, v[:-1]], axis=0)

    def near3(v):
        return [along_xz(v[0], 1) + v[1] + down(v[1]), along_xz(v[1], 1) + v[0] + up(v[0])]

    def near_coarse(v, s):
        return along_xz(v, s) + up(v) + down(v)

    km5 = km[:ny // 2]
    for vec in range(4):
        b = [spread(1, 2 * vec + q) for q in range(2)]
        g = [b[q] * inv3[q] for q in range(2)]
        near = near3(g)
        v = [1.2 * g[q] + km * near[q] for q in range(2)]
        near = near3(v)
        third = [0.2 * v[q] + g[q] + km * near[q] for q in range(2)]
        r = [b[q] - cc3[q] * (6.0 * v[q] - near[q]) for q in range(2)]
        b4 = coarsen_gathered(jnp.where(inside, r[0] + r[1], 0.0), 1)
        g4 = b4 * inv4[...]
        v4 = 1.2 * g4 + km * near_coarse(g4, 2)
        n4 = near_coarse(v4, 2)
        third4 = 0.2 * v4 + g4 + km * n4
        r4_ = b4 - cc4[...] * (6.0 * v4 - n4)
        r4_ = jnp.where(inside, r4_, 0.0).reshape(ny // 2, 2, nx, Z)
        g5 = coarsen_gathered(r4_[:, 0] + r4_[:, 1], 2) * inv5[...]
        v5 = g5
        for _ in range(3):
            v5 = 0.2 * v5 + g5 + km5 * near_coarse(v5, 4)
        p4 = jnp.stack([v5, v5], axis=1).reshape(ny, nx, Z)
        e4 = third4 + 0.2 * p4 + km * near_coarse(p4, 2)
        xz = along_xz(e4, 1)
        ebuf[2 * vec, 1:ny + 1, 8:8 + nx] = third[0] + 0.2 * e4 + km * (xz + e4 + down(e4))
        ebuf[2 * vec + 1, 1:ny + 1, 8:8 + nx] = third[1] + 0.2 * e4 + km * (xz + e4 + up(e4))

    receive(T2, s2, 2)
    around = [(dx, dy) for dx in (-1, 0, 1) for dy in (0, -1, 1)]
    stacked = jnp.concatenate([ebuf[:, gy + 1 + dy, pl.ds(8 + gx + dx, 1), :].reshape(8, Z) for dx, dy in around], axis=0)
    li, lj = iota((Z, Z), 0), iota((Z, Z), 1)
    after = lj < 64
    maps = [li == 32 + lj // 8, (li == 31 + (lj + 4) // 8) | (li == 32 + (lj + 4) // 8),
            li == jnp.where(after, 48, 31), (li == jnp.where(after, 47, 31)) | (li == jnp.where(after, 48, 32))]
    spread_rows = [lax.dot_general(stacked, m.astype(F32), (((1,), (0,)), ((), ())), precision=HIGH,
                                   preferred_element_type=F32) for m in maps]

    def cell(kind, vec, y2, dx, dy=0):
        i = 8 * around.index((dx, dy)) + 2 * vec + y2
        return wide(spread_rows[kind][i:i + 1])

    def flag(cond):
        return jnp.where(cond, 1.0, 0.0).astype(F32)
    x_in, y_in = (flag(gx > 0), flag(gx < nx - 1)), (flag(gy > 0), flag(gy < ny - 1))
    z_in = jnp.where(lane8 < 64, flag(gz < nz - 1), flag(gz > 0))
    ends = jnp.where(row8 == 0, zr[0, T2, 0], jnp.where(row8 == 1, zr[1, T2, 0], 0.0))
    put = (((row8 == 0) & (lane8 >= 64)) | ((row8 == 1) & (lane8 < 64))).astype(F32)
    third_out = lax.dot_general(ends, put, (((0,), (0,)), ((), ())), precision=HIGH, preferred_element_type=F32)
    third_out = third_out.reshape(4, 2, Y, Z)
    for vec in range(4):
        for dx, others in ((0, (-1, 1)), (-1, (0,)), (1, (0,))):
            for kind in (0, 2) if dx == 0 else (0,):
                a = [cell(kind, vec, y2, dx) for y2 in range(2)]
                mid = a[0] + a[1]
                y_sum = [jnp.where(row8 < 4, cell(kind, vec, 1, dx, -1) + a[0], mid),
                         jnp.where(row8 < 4, mid, a[1] + cell(kind, vec, 0, dx, 1))]
                for h in range(2):
                    part = slice(8 * h, 8 * h + 8)
                    base = 0.2 * a[h] + KS * (y_sum[h] + cell(kind + 1, vec, h, dx) + a[h])
                    for x, other in enumerate(others):
                        value = base + KS * cell(kind, vec, h, other)
                        if dx:
                            side = 0 if dx < 0 else 1
                            xr[side, C2, vec, part] = xr[side, T2, vec, part] + x_in[side] * value
                        elif kind == 0:
                            e2[vec, x, part] = s2[vec, x, part] + value
                        else:
                            beyond[vec, x, part] = third_out[vec, x, part] + z_in * value
        for side, dy, y2 in ((0, -1, 1), (1, 1, 0)):
            b = cell(0, vec, y2, 0, dy)[0:1]
            base = 0.2 * b + KS * (2.0 * b + cell(0, vec, 1 - y2, 0)[0:1] + cell(1, vec, y2, 0, dy)[0:1])
            for x, dx in enumerate((-1, 1)):
                value = base + KS * cell(0, vec, y2, dx, dy)[0:1]
                yr[side, C2, vec, x] = yr[side, T2, vec, x] + y_in[side] * value

    corrected(C2, e2, s1, e1, 2, 2)
    send(C1, e1, 4)
    receive(C1, e1, 4)
    corrected(C1, e1, s0, e0, 4, 1)
    send(C0, e0, 8)
    receive(C0, e0, 8)
    for c in range(4):
        x, near = neighbours(C0, e0, 8, 1, c)
        oper[c:c + 1] = c_fine * (6.0 * x - near)
    for copy, sends in sent:
        @pl.when(sends)
        def _():
            copy.wait_send()
    for k in range(2):
        for copy, sends, _ in deep_copies(k):
            @pl.when(sends)
            def _():
                copy.wait_send()


def write_out(*refs):
    sems = refs[-1]
    copies = [pltpu.make_async_copy(refs[i], refs[5 + i], sems.at[i]) for i in range(5)]
    for copy in copies:
        copy.start()
    for copy in copies:
        copy.wait()


def per_device(shape, old_basis, previous, incoming, coefficient):
    nx, ny, nz = shape
    big = pltpu.VMEM((4, 8, 16, 128), F32)
    mid = pltpu.VMEM((4, 4, 16, 128), F32)
    low = pltpu.VMEM((4, 2, 16, 128), F32)
    dma = pltpu.SemaphoreType.DMA
    vm = lambda *s: pltpu.VMEM(s, F32)
    whole = jax.ShapeDtypeStruct((4, 8, 16, 128), F32)
    small = jax.ShapeDtypeStruct((4, 4), F32)
    held = (vm(4, 8, 16, 128), vm(4, 4), vm(4, 4), vm(4, 8, 16, 128), vm(4, 8, 16, 128))
    any_spec = pl.BlockSpec(memory_space=pl.ANY)
    vmem_spec = pl.BlockSpec(memory_space=pltpu.VMEM)
    results = pl.pallas_call(
        functools.partial(kernel, nx, ny, nz),
        out_shape=held,
        in_specs=[any_spec] * 4,
        out_specs=(vmem_spec,) * 5,
        scratch_shapes=[
            big, big, big, vm(8, 16, 128),
            big, big, big, mid, mid, mid, mid, low, low, low, low, low, mid, vm(4, 16, 128), vm(2, 16, 128), low,
            vm(2, 9, 4, 8, 128), vm(2, 9, 4, 8, 128), vm(2, 10, 4, 16, 128), vm(2, 9, 4, 8, 1, 128),
            vm(2, 10, 4, 8, 1, 128), vm(2, 9, 4, 1, 128), vm(2, 9, 4, 1, 128),
            vm(2, 1, 128), vm(2, nx, 1, 128), vm(2, nx, 128), vm(2, 5, ny, nx, 128), vm(1, 128), vm(nz, 1, 128),
            vm(2, ny, nx, 128), vm(2, ny, nx, 128), vm(ny, nx, 128), vm(ny, nx, 128), vm(ny // 2, nx, 128),
            vm(8, ny + 2, nx + 16, 128),
            dma((4,)), dma((2, 9)), dma((2, 9)), dma((2, 9)), dma((2, 9)), dma((2, 9)), dma((2, 9)),
            dma((2, nx - 1)), dma((2, nx - 1)), dma((2, 5 * ny - 1)), dma((2, 5 * ny - 1)),
            dma((nz - 1,)), dma((nz - 1,)),
        ],
        compiler_params=pltpu.CompilerParams(collective_id=0, has_side_effects=True),
    )(old_basis, previous, incoming, coefficient)
    return pl.pallas_call(
        write_out,
        out_shape=(whole, small, small, whole, whole),
        in_specs=[vmem_spec] * 5,
        out_specs=(any_spec,) * 5,
        scratch_shapes=[dma((5,))],
    )(*[pltpu.with_memory_space_constraint(r, pltpu.VMEM) for r in results])


def solution(mesh):
    shape = (mesh.shape["gx"], mesh.shape["gy"], mesh.shape["gz"])
    split = P(None, "gx", "gy", "gz")
    return jax.shard_map(
        functools.partial(per_device, shape), mesh=mesh,
        in_specs=(split, split, split, P("gx", "gy", "gz")),
        out_specs=(split, P(), P(), split, split), check_vma=False,
    )
```

```python
import functools

import jax
import jax.numpy as jnp
from jax import lax
from jax.experimental import pallas as pl
from jax.experimental.pallas import tpu as pltpu
from jax.sharding import PartitionSpec as P

OMEGA = 0.8
HIGH = lax.Precision.HIGHEST
MESH = pl.DeviceIdType.MESH
KS = OMEGA / 6.0
F32 = jnp.float32
ANY = pl.ANY

G0, V0, G1, V1, G2, V2, T2, C1, C0, C2 = range(10)


def iota(shape, dim):
    return lax.broadcasted_iota(jnp.int32, shape, dim)


def roll(x, shift, axis):
    n = x.shape[axis]
    shift = shift % n
    return x if shift == 0 else pltpu.roll(x, shift, axis)


def partner_sum(x, axis, s):
    low = (iota(x.shape, axis) & s) == 0
    return x + jnp.where(low, roll(x, x.shape[axis] - s, axis), roll(x, s, axis))


def coarsen(x, s):
    pairs = x.reshape(*x.shape[:-3], x.shape[-3] // 2, 2, *x.shape[-2:])
    x = pairs[..., 0, :, :] + pairs[..., 1, :, :]
    x = partner_sum(x, x.ndim - 2, s)
    return partner_sum(x, x.ndim - 1, s) * 0.125


def kernel(nx, ny, nz, old_hbm, prev_hbm, inc_hbm, coef_hbm,
           ortho, proj_ref, tri_ref, e0, oper,
           old, prev, inc, coef,
           g0, v0, s0, b1, g1, v1, s1, b2, g2, v2, s2, e2, e1, c1, c2, beyond,
           xs, xc, xr, ys, yr, zs, zr, row_s, row_r, line_b, zb, planes, passed, all_planes,
           cc3, inv3, cc4, inv4, inv5, ebuf,
           in_sem, x_send, x_recv, y_send, y_recv, z_send, z_recv,
           ax_send, ax_recv, az_send, az_recv, ag_send, ag_recv):
    gx, gy, gz = lax.axis_index("gx"), lax.axis_index("gy"), lax.axis_index("gz")
    X, Y, Z = 8, 16, 128

    def at(dx=0, dy=0, dz=0):
        return (lax.rem(gx + dx + nx, nx), lax.rem(gy + dy + ny, ny), lax.rem(gz + dz + nz, nz))

    loads = [
        pltpu.make_async_copy(src, dst, in_sem.at[i])
        for i, (src, dst) in enumerate(((coef_hbm, coef), (inc_hbm, inc), (old_hbm, old), (prev_hbm, prev)))
    ]
    for load in loads:
        load.start()

    barrier = pltpu.get_barrier_semaphore()
    for d in range(1, nx):
        pl.semaphore_signal(barrier, inc=1, device_id=at(dx=d), device_id_type=MESH)
    partners = jnp.int32(nx - 1)
    for dz in range(-2, 3):
        reach = (gz + dz >= 0) & (gz + dz < nz)
        partners = partners + jnp.where(reach, ny - (dz == 0), 0)

        @pl.when(reach)
        def _():
            for dy in range(1 if dz == 0 else 0, ny):
                pl.semaphore_signal(barrier, inc=1, device_id=at(dy=dy, dz=dz), device_id_type=MESH)

    lane8, row8 = iota((8, Z), 1), iota((8, Z), 0)
    wide = lambda a: jnp.broadcast_to(a, (8, Z))
    def copy_to(src, dst, ssem, rsem, to):
        return pltpu.make_async_remote_copy(src_ref=src, dst_ref=dst, send_sem=ssem, recv_sem=rsem, device_id=to,
                                            device_id_type=MESH)

    def faces(e, f, n, axis):
        out = []
        for side, d in ((0, 1), (1, -1)):
            if axis == 0:
                if n == 8:
                    src, dst = f.at[:, (n - 1) if side == 0 else 0], xr.at[side, e]
                else:
                    src, dst = xs.at[side, e, pl.ds(0, n)], xc.at[side, e, pl.ds(0, n)]
                copy = copy_to(src, dst, x_send.at[side, e], x_recv.at[side, e], at(dx=d))
                place, count = gx, nx
            elif axis == 1:
                copy = copy_to(ys.at[side, e, :, pl.ds(0, n)], yr.at[side, e, :, pl.ds(0, n)], y_send.at[side, e],
                               y_recv.at[side, e], at(dy=d))
                place, count = gy, ny
            else:
                copy = copy_to(zs.at[side, e], zr.at[side, e], z_send.at[side, e],
                               z_recv.at[side, e], at(dz=d))
                place, count = gz, nz
            out.append((copy, (place + d >= 0) & (place + d < count), (place - d >= 0) & (place - d < count)))
        return out

    sent = []

    def start(e, f, n, axis):
        for copy, sends, _ in faces(e, f, n, axis):
            sent.append((copy, sends))

            @pl.when(sends)
            def _():
                copy.start()

    def send(e, f, n):
        for side, x in ((0, n - 1), (1, 0)):
            for v in range(4):
                if n == 4:
                    xs[side, e, v] = f[v, x, pl.ds(0, 8, stride=2), :]
                elif n == 2:
                    xs[side, e, v // 2, 4 * (v % 2):4 * (v % 2) + 4] = f[v, x, pl.ds(0, 4, stride=4), :]
        start(e, f, n, 0)
        ys[0, e, :, 0:n] = f[:, :, Y - 1:Y, :]
        ys[1, e, :, 0:n] = f[:, :, 0:1, :]
        start(e, f, n, 1)
        packed = [jnp.zeros((8, Z), F32)] * 2
        for i in range(8 * n):
            tile = f[i // (2 * n), i // 2 % n, 8 * (i % 2):8 * (i % 2) + 8]
            here = lane8 == i
            packed = [jnp.where(here, tile[:, x:x + 1], p) for x, p in zip((Z - 1, 0), packed)]
        zs[0, e] = packed[0]
        zs[1, e] = packed[1]
        start(e, f, n, 2)

    def receive(e, f, n):
        for axis in range(3):
            for copy, _, receives in faces(e, f, n, axis):
                @pl.when(receives)
                def _():
                    copy.wait_recv()
        if n < 8:
            for side in range(2):
                for v in range(4):
                    if n == 4:
                        half = xc[side, e, v]
                        for i in range(2):
                            xr[side, e, v, pl.ds(i, 8, stride=2), :] = half
                    else:
                        half = xc[side, e, v // 2, 4 * (v % 2):4 * (v % 2) + 4]
                        for i in range(4):
                            xr[side, e, v, pl.ds(i, 4, stride=4), :] = half

    def z_halo(e, side, first, count):
        packed = zr[side, e]
        return jnp.concatenate([jnp.broadcast_to(packed[:, i:i + 1], (8, Z)) for i in range(first, first + count)], axis=0)

    def along_yz(e, f, n, s, c):
        per = 8 // n
        shape = (per, n, Y, Z)
        x = f[c * per:(c + 1) * per]
        row, lane = iota(shape, 2), iota(shape, 3)
        lo, hi = (yr[side, e, c * per:(c + 1) * per, 0:n] for side in (0, 1))
        total = jnp.where(row >= s, roll(x, s, 2), lo) + jnp.where(row < Y - s, roll(x, Y - s, 2), hi)
        if e == C2:
            out = beyond[c * per:(c + 1) * per]
            return x, (total + jnp.where(lane >= s, roll(x, s, 3), roll(out, s, 3))
                       + jnp.where(lane < Z - s, roll(x, Z - s, 3), roll(out, Z - s, 3)))
        lo, hi = (z_halo(e, side, 16 * c, 16).reshape(shape) for side in (0, 1))
        return x, (total + jnp.where(lane >= s, roll(x, s, 3), lo)
                   + jnp.where(lane < Z - s, roll(x, Z - s, 3), hi))

    def x_ends(e, n, c):
        per = 8 // n
        return (xr[side, e, c * per:(c + 1) * per][:, None] for side in (0, 1))

    def neighbours(e, f, n, s, c):
        x, total = along_yz(e, f, n, s, c)
        lo, hi = x_ends(e, n, c)
        if n > 1:
            lo = jnp.concatenate([lo, x[:, :-1]], axis=1)
            hi = jnp.concatenate([x[:, 1:], hi], axis=1)
        return x, total + lo + hi

    def second_sweep(e, g, v, n, s):
        receive(e, g, n)
        per = 8 // n
        for c in range(n // 2):
            x, near = neighbours(e, g, n, s, c)
            v[c * per:(c + 1) * per] = 1.2 * x + KS * near

    def residual(e, b, c_hat, g, v, third, n, s, put):
        receive(e, v, n)
        per = 8 // n
        for c in range(n // 2):
            part = slice(c * per, (c + 1) * per)
            x, near = neighbours(e, v, n, s, c)
            third[part] = 0.2 * x + g[part] + KS * near
            put(part, coarsen(b[part] - c_hat * (6.0 * x - near), s))

    def corrected(e, coarse, third, out, n, s):
        per = 8 // n
        for c in range(n // 2):
            part = slice(c * per, (c + 1) * per)
            x, near = along_yz(e, coarse, n, s, c)
            near = near + x
            lo, hi = x_ends(e, n, c)
            if n > 1:
                lo = jnp.concatenate([lo, x[:, :-1]], axis=1)
                hi = jnp.concatenate([x[:, 1:], hi], axis=1)
            both = jnp.stack([0.2 * x + KS * (near + lo), 0.2 * x + KS * (near + hi)], axis=2)
            out[part] = third[part] + both.reshape(per, 2 * n, Y, Z)

    def line_copies(k):
        return [pltpu.make_async_remote_copy(
            src_ref=row_s.at[k], dst_ref=row_r.at[k, gx], send_sem=ax_send.at[k, d - 1], recv_sem=ax_recv.at[k, d - 1],
            device_id=at(dx=d), device_id_type=MESH) for d in range(1, nx)]

    slabs = [(dy, dz) for dz in (0, -1, 1, -2, 2) for dy in range(ny) if dy or dz]

    def deep_copies(k):
        return [(copy_to(line_b.at[k], zb.at[k, 2 - dz, gy], az_send.at[k, i], az_recv.at[k, i], at(dy=dy, dz=dz)),
                 (gz + dz >= 0) & (gz + dz < nz), (gz - dz >= 0) & (gz - dz < nz)) for i, (dy, dz) in enumerate(slabs)]

    def start_line(k, row):
        row_s[k] = row
        row_r[k, gx] = row
        for copy in line_copies(k):
            copy.start()

    def start_deep(k):
        for copy in line_copies(k):
            copy.wait()
        line_b[k] = row_r[k].reshape(nx, Z)
        for copy, sends, _ in deep_copies(k):
            @pl.when(sends)
            def _():
                copy.start()
        zb[k, 2, gy] = line_b[k]

    def finish_deep(k):
        for copy, _, receives in deep_copies(k):
            @pl.when(receives)
            def _():
                copy.wait_recv()

    rounds = (nz - 2) // 2

    def chain_copies(i):
        out = []
        for side, d in ((0, 2), (1, -2)):
            src = planes.at[pl.ds(0 if side == 0 else 3, 2)] if i == 0 else passed.at[side, i - 1]
            copy = copy_to(src, passed.at[side, i], ag_send.at[side, i], ag_recv.at[side, i], at(dz=d))
            near_row = 3 + 2 * i
            if side == 0:
                out.append((copy, (gz + d < nz) & (gz + d - near_row >= 0), gz - near_row >= 0))
            else:
                out.append((copy, (gz + d >= 0) & (gz + d + near_row < nz), gz + near_row < nz))
        return out

    def chain_start(i):
        if i >= rounds:
            return
        for copy, sends, _ in chain_copies(i):
            @pl.when(sends)
            def _():
                copy.start()

    def chain_wait(i):
        if i >= rounds:
            return
        for copy, _, receives in chain_copies(i):
            @pl.when(receives)
            def _():
                copy.wait_recv()

    def chain_next(i):
        chain_wait(i - 1)
        chain_start(i)

    def to_row(blocks):
        q = blocks.shape[0]
        rows = jnp.zeros((8, Z), F32)
        for i in range(q):
            rows = jnp.where(row8 == i, blocks[i], rows)
        pick = (iota((Z, Z), 0) == 8 * (iota((Z, Z), 1) % 16)).astype(F32)
        rows = lax.dot_general(rows, pick, (((1,), (0,)), ((), ())), precision=HIGH, preferred_element_type=F32)
        return jnp.sum(jnp.where(lane8 // 16 == row8, rows, 0.0), axis=0, keepdims=True)

    def spread(k, q):
        shape = (ny, nx, Z)
        group = iota(shape, 2) // 16
        out = jnp.zeros(shape, F32)
        for i in range(5):
            out = jnp.where(group == i, roll(zb[k, i], 16 * (i - q), 2), out)
        return out

    loads[0].wait()
    loads[1].wait()
    c_fine = coef[...]
    scale = KS / c_fine
    for v in range(4):
        g0[v] = inc[v] * scale
    pl.semaphore_wait(barrier, partners)
    send(G0, g0, 8)
    for cond, buf, side in ((gx == 0, xr, 0), (gx == nx - 1, xr, 1), (gx == 0, xc, 0), (gx == nx - 1, xc, 1), (gy == 0, yr, 0), (gy == ny - 1, yr, 1),
                            (gz == 0, zr, 0), (gz == nz - 1, zr, 1)):
        @pl.when(cond)
        def _():
            buf[side] = jnp.zeros(buf.shape[1:], F32)
    for side in range(2):
        for i in range((nz - 2) // 2):
            missing = (gz - 3 - 2 * i < 0) if side == 0 else (gz + 3 + 2 * i >= nz)

            @pl.when(missing)
            def _():
                passed[side, i] = jnp.zeros(passed.shape[2:], F32)
    for d in (-2, -1, 1, 2):
        @pl.when((gz + d < 0) | (gz + d >= nz))
        def _():
            zb[:, 2 + d] = jnp.zeros((2,) + zb.shape[2:], F32)

    ebuf[:, 0] = jnp.zeros(ebuf.shape[:1] + ebuf.shape[2:], F32)
    ebuf[:, ny + 1] = jnp.zeros(ebuf.shape[:1] + ebuf.shape[2:], F32)
    ebuf[:, 1:ny + 1, 0:8] = jnp.zeros((8, ny, 8, Z), F32)
    ebuf[:, 1:ny + 1, 8 + nx:] = jnp.zeros((8, ny, 8, Z), F32)

    c1[...] = coarsen(c_fine, 1)
    c2[...] = coarsen(c1[...], 2)
    c3 = coarsen(c2[...], 4)


    loads[2].wait()
    loads[3].wait()
    pairs = [("p", m, j) for m in range(4) for j in range(4)]
    pairs += [("s", i, j) for i in range(4) for j in range(i, 4)]
    pairs += [("c", i, j) for i in range(4) for j in range(i, 4)]
    sums = [None] * len(pairs)
    for x in range(X):
        vo = [old[m, x] for m in range(4)]
        vp = [prev[m, x] for m in range(4)]
        for p, (kind, i, j) in enumerate(pairs):
            a = (vp if kind == "s" else vo)[i]
            b = (vo if kind == "c" else vp)[j]
            ab = a * b
            ab = ab[0:8] + ab[8:16]
            sums[p] = ab if sums[p] is None else sums[p] + ab
    rows = [jnp.sum(a, axis=0, keepdims=True) for a in sums] + [jnp.zeros((4, Z), F32)]
    rows = jnp.sum(jnp.concatenate(rows, axis=0), axis=1, keepdims=True)
    at_lane = iota((40, Z), 1) == iota((40, Z), 0) + 64
    gram_row = jnp.sum(jnp.where(at_lane, rows, 0.0), axis=0, keepdims=True)
    start_line(0, to_row(c3.reshape(2, 8, Z)) + gram_row)

    second_sweep(G0, g0, v0, 8, 1)
    send(V0, v0, 8)
    start_deep(0)

    def put_b1(part, r):
        b1[part] = r
        g1[part] = r * scale1
    scale1 = (4.0 * KS) / c1[...]
    residual(V0, inc, c_fine, g0, v0, s0, 8, 1, put_b1)
    send(G1, g1, 4)

    second_sweep(G1, g1, v1, 4, 2)
    send(V1, v1, 4)
    scale2 = (16.0 * KS) / c2[...]

    def put_b2(part, r):
        b2[part] = r
        g2[part] = r * scale2
    residual(V1, b1, 0.25 * c1[...], g1, v1, s1, 4, 2, put_b2)
    send(G2, g2, 2)
    finish_deep(0)
    for i in range(5):
        planes[i] = jnp.sum(zb[0, i].reshape(ny * nx, Z), axis=0, keepdims=True)
    chain_start(0)
    second_sweep(G2, g2, v2, 2, 4)
    send(V2, v2, 2)
    chain_next(1)
    held = []
    residual(V2, b2, 0.0625 * c2[...], g2, v2, s2, 2, 4, lambda part, r: held.append(r))
    start_line(1, to_row(held[0].reshape(8, 8, Z)))
    send(T2, s2, 2)
    chain_next(2)

    shape = (ny, nx, Z)
    lanes = iota(shape, 2)
    place = (gz - 2) * 16 + lanes
    inside = (place >= 0) & (place < nz * 16) & (lanes < 80)
    km = jnp.where(inside, KS, 0.0)
    c3g = [jnp.where(inside, spread(0, q), 1.0) for q in range(2)]
    for q in range(2):
        cc3[q] = (1.0 / 64) * c3g[q]
        inv3[q] = jnp.where(inside, (64.0 * KS) / c3g[q], 0.0)

    def coarsen_gathered(x, s):
        x = partner_sum(x, 1, s)
        return partner_sum(x, 2, s) * 0.125
    c4g = coarsen_gathered(c3g[0] + c3g[1], 1)
    cc4[...] = (1.0 / 256) * c4g
    inv4[...] = jnp.where(inside, (256.0 * KS) / c4g, 0.0)
    halved = c4g.reshape(ny // 2, 2, nx, Z)
    c5g = coarsen_gathered(halved[:, 0] + halved[:, 1], 2)
    inv5[...] = jnp.where(inside[:ny // 2], (1024.0 * KS) / c5g, 0.0)

    start_deep(1)

    chain_next(3)
    finish_deep(1)
    chain_next(4)

    rows_i = iota(shape, 1)
    zero = jnp.zeros((1, nx, Z), F32)

    def along_xz(v, s):
        r = rows_i[:v.shape[0]]
        out = jnp.where(r >= s, roll(v, s, 1), 0.0) + jnp.where(r < nx - s, roll(v, nx - s, 1), 0.0)
        return out + roll(v, s, 2) + roll(v, Z - s, 2)

    def up(v):
        return zero if v.shape[0] == 1 else jnp.concatenate([v[1:], zero], axis=0)

    def down(v):
        return zero if v.shape[0] == 1 else jnp.concatenate([zero, v[:-1]], axis=0)

    def near3(v):
        return [along_xz(v[0], 1) + v[1] + down(v[1]), along_xz(v[1], 1) + v[0] + up(v[0])]

    def near_coarse(v, s):
        return along_xz(v, s) + up(v) + down(v)

    km5 = km[:ny // 2]
    for vec in range(4):
        b = [spread(1, 2 * vec + q) for q in range(2)]
        g = [b[q] * inv3[q] for q in range(2)]
        near = near3(g)
        v = [1.2 * g[q] + km * near[q] for q in range(2)]
        near = near3(v)
        third = [0.2 * v[q] + g[q] + km * near[q] for q in range(2)]
        r = [b[q] - cc3[q] * (6.0 * v[q] - near[q]) for q in range(2)]
        b4 = coarsen_gathered(jnp.where(inside, r[0] + r[1], 0.0), 1)
        g4 = b4 * inv4[...]
        v4 = 1.2 * g4 + km * near_coarse(g4, 2)
        n4 = near_coarse(v4, 2)
        third4 = 0.2 * v4 + g4 + km * n4
        r4_ = b4 - cc4[...] * (6.0 * v4 - n4)
        r4_ = jnp.where(inside, r4_, 0.0).reshape(ny // 2, 2, nx, Z)
        g5 = coarsen_gathered(r4_[:, 0] + r4_[:, 1], 2) * inv5[...]
        v5 = g5
        for _ in range(3):
            v5 = 0.2 * v5 + g5 + km5 * near_coarse(v5, 4)
        p4 = jnp.stack([v5, v5], axis=1).reshape(ny, nx, Z)
        e4 = third4 + 0.2 * p4 + km * near_coarse(p4, 2)
        xz = along_xz(e4, 1)
        ebuf[2 * vec, 1:ny + 1, 8:8 + nx] = third[0] + 0.2 * e4 + km * (xz + e4 + down(e4))
        ebuf[2 * vec + 1, 1:ny + 1, 8:8 + nx] = third[1] + 0.2 * e4 + km * (xz + e4 + up(e4))

    receive(T2, s2, 2)
    around = [(dx, dy) for dx in (-1, 0, 1) for dy in (0, -1, 1)]
    stacked = jnp.concatenate([ebuf[:, gy + 1 + dy, pl.ds(8 + gx + dx, 1), :].reshape(8, Z) for dx, dy in around], axis=0)
    li, lj = iota((Z, Z), 0), iota((Z, Z), 1)
    after = lj < 64
    maps = [li == 32 + lj // 8, (li == 31 + (lj + 4) // 8) | (li == 32 + (lj + 4) // 8),
            li == jnp.where(after, 48, 31), (li == jnp.where(after, 47, 31)) | (li == jnp.where(after, 48, 32))]
    spread_rows = [lax.dot_general(stacked, m.astype(F32), (((1,), (0,)), ((), ())), precision=HIGH,
                                   preferred_element_type=F32) for m in maps]

    def cell(kind, vec, y2, dx, dy=0):
        i = 8 * around.index((dx, dy)) + 2 * vec + y2
        return wide(spread_rows[kind][i:i + 1])

    def flag(cond):
        return jnp.where(cond, 1.0, 0.0).astype(F32)
    x_in, y_in = (flag(gx > 0), flag(gx < nx - 1)), (flag(gy > 0), flag(gy < ny - 1))
    z_in = jnp.where(lane8 < 64, flag(gz < nz - 1), flag(gz > 0))
    third_out = jnp.where(iota((128, Z), 1) < 64, z_halo(T2, 1, 0, 16), z_halo(T2, 0, 0, 16)).reshape(4, 2, Y, Z)
    for vec in range(4):
        for dx, others in ((0, (-1, 1)), (-1, (0,)), (1, (0,))):
            for kind in (0, 2) if dx == 0 else (0,):
                a = [cell(kind, vec, y2, dx) for y2 in range(2)]
                mid = a[0] + a[1]
                y_sum = [jnp.where(row8 < 4, cell(kind, vec, 1, dx, -1) + a[0], mid),
                         jnp.where(row8 < 4, mid, a[1] + cell(kind, vec, 0, dx, 1))]
                for h in range(2):
                    part = slice(8 * h, 8 * h + 8)
                    base = 0.2 * a[h] + KS * (y_sum[h] + cell(kind + 1, vec, h, dx) + a[h])
                    for x, other in enumerate(others):
                        value = base + KS * cell(kind, vec, h, other)
                        if dx:
                            side = 0 if dx < 0 else 1
                            xr[side, C2, vec, part] = xr[side, T2, vec, part] + x_in[side] * value
                        elif kind == 0:
                            e2[vec, x, part] = s2[vec, x, part] + value
                        else:
                            beyond[vec, x, part] = third_out[vec, x, part] + z_in * value
        for side, dy, y2 in ((0, -1, 1), (1, 1, 0)):
            b = cell(0, vec, y2, 0, dy)[0:1]
            base = 0.2 * b + KS * (2.0 * b + cell(0, vec, 1 - y2, 0)[0:1] + cell(1, vec, y2, 0, dy)[0:1])
            for x, dx in enumerate((-1, 1)):
                value = base + KS * cell(0, vec, y2, dx, dy)[0:1]
                yr[side, C2, vec, x] = yr[side, T2, vec, x] + y_in[side] * value

    corrected(C2, e2, s1, e1, 2, 2)
    send(C1, e1, 4)
    chain_next(5)
    receive(C1, e1, 4)
    chain_next(6)
    corrected(C1, e1, s0, e0, 4, 1)
    send(C0, e0, 8)
    for i in range(7, rounds + 1):
        chain_next(i)
    for i in range(5):
        all_planes[gz + nz + i - 2] = planes[i]
    for i in range(rounds):
        for j in range(2):
            all_planes[gz + nz - 4 - 2 * i + j] = passed[0, i, j]
            all_planes[gz + nz + 3 + 2 * i + j] = passed[1, i, j]
    line = jnp.sum(all_planes[nz:2 * nz].reshape(nz, Z), axis=0, keepdims=True)
    column = jnp.sum(jnp.where(at_lane, line, 0.0), axis=1, keepdims=True)
    column = column * (1.0 / float(nx * ny * nz * X * Y * Z))
    value = {key: column[p:p + 1] for p, key in enumerate(pairs)}
    for kind in "sc":
        for i in range(4):
            for j in range(i):
                value[kind, i, j] = value[kind, j, i]
    proj = [[value["p", m, j] for j in range(4)] for m in range(4)]
    mixed = [[sum(value["c", m, n] * proj[n][j] for n in range(4)) for j in range(4)] for m in range(4)]
    low = [[None] * 4 for _ in range(4)]
    inverse = [[None] * 4 for _ in range(4)]
    for j in range(4):
        for i in range(j, 4):
            g = value["s", i, j] + sum(proj[m][i] * (mixed[m][j] - 2.0 * proj[m][j]) for m in range(4))
            for k in range(j):
                g = g - low[i][k] * low[j][k]
            low[i][j] = jnp.sqrt(g) if i == j else g / low[j][j]
    for j in range(4):
        inverse[j][j] = 1.0 / low[j][j]
        for i in range(j + 1, 4):
            inverse[i][j] = -sum(low[i][k] * inverse[k][j] for k in range(j, i)) * (1.0 / low[i][i])
    r4, l4 = iota((4, 4), 0), iota((4, 4), 1)
    out_p, out_t = jnp.zeros((4, 4), F32), jnp.zeros((4, 4), F32)
    for i in range(4):
        for j in range(4):
            here = (r4 == i) & (l4 == j)
            out_p = jnp.where(here, proj[i][j], out_p)
            if j >= i:
                out_t = jnp.where(here, low[j][i], out_t)
    proj_ref[...] = out_p
    tri_ref[...] = out_t
    proj_w = [[wide(a) for a in line_] for line_ in proj]
    inv_w = [[wide(inverse[j][i]) if i <= j else None for i in range(4)] for j in range(4)]
    for x in range(X):
        for h in range(2):
            part = slice(8 * h, 8 * h + 8)
            vo = [old[m, x, part] for m in range(4)]
            rem = [prev[j, x, part] - sum(proj_w[m][j] * vo[m] for m in range(4)) for j in range(4)]
            for j in range(4):
                ortho[j, x, part] = sum(inv_w[j][i] * rem[i] for i in range(j + 1))

    receive(C0, e0, 8)
    for c in range(4):
        x, near = neighbours(C0, e0, 8, 1, c)
        oper[c:c + 1] = c_fine * (6.0 * x - near)
    for copy, sends in sent:
        @pl.when(sends)
        def _():
            copy.wait_send()
    for i in range(rounds):
        sent += [(copy, sends) for copy, sends, _ in chain_copies(i)]
    for copy, sends in sent[-2 * rounds:]:
        @pl.when(sends)
        def _():
            copy.wait_send()
    for k in range(2):
        for copy, sends, _ in deep_copies(k):
            @pl.when(sends)
            def _():
                copy.wait_send()


def write_out(*refs):
    sems = refs[-1]
    copies = [pltpu.make_async_copy(refs[i], refs[5 + i], sems.at[i]) for i in range(5)]
    for copy in copies:
        copy.start()
    for copy in copies:
        copy.wait()


def per_device(shape, old_basis, previous, incoming, coefficient):
    nx, ny, nz = shape
    big = pltpu.VMEM((4, 8, 16, 128), F32)
    mid = pltpu.VMEM((4, 4, 16, 128), F32)
    low = pltpu.VMEM((4, 2, 16, 128), F32)
    dma = pltpu.SemaphoreType.DMA
    vm = lambda *s: pltpu.VMEM(s, F32)
    whole = jax.ShapeDtypeStruct((4, 8, 16, 128), F32)
    small = jax.ShapeDtypeStruct((4, 4), F32)
    held = (vm(4, 8, 16, 128), vm(4, 4), vm(4, 4), vm(4, 8, 16, 128), vm(4, 8, 16, 128))
    any_spec = pl.BlockSpec(memory_space=pl.ANY)
    vmem_spec = pl.BlockSpec(memory_space=pltpu.VMEM)
    results = pl.pallas_call(
        functools.partial(kernel, nx, ny, nz),
        out_shape=held,
        in_specs=[any_spec] * 4,
        out_specs=(vmem_spec,) * 5,
        scratch_shapes=[
            big, big, big, vm(8, 16, 128),
            big, big, big, mid, mid, mid, mid, low, low, low, low, low, mid, vm(4, 16, 128), vm(2, 16, 128), low,
            vm(2, 9, 4, 8, 128), vm(2, 9, 4, 8, 128), vm(2, 10, 4, 16, 128), vm(2, 9, 4, 8, 1, 128),
            vm(2, 10, 4, 8, 1, 128), vm(2, 9, 8, 128), vm(2, 9, 8, 128),
            vm(2, 1, 128), vm(2, nx, 1, 128), vm(2, nx, 128), vm(2, 5, ny, nx, 128), vm(5, 1, 128), vm(2, (nz - 2) // 2, 2, 1, 128), vm(3 * nz, 1, 128),
            vm(2, ny, nx, 128), vm(2, ny, nx, 128), vm(ny, nx, 128), vm(ny, nx, 128), vm(ny // 2, nx, 128),
            vm(8, ny + 2, nx + 16, 128),
            dma((4,)), dma((2, 9)), dma((2, 9)), dma((2, 9)), dma((2, 9)), dma((2, 9)), dma((2, 9)),
            dma((2, nx - 1)), dma((2, nx - 1)), dma((2, 5 * ny - 1)), dma((2, 5 * ny - 1)),
            dma((2, (nz - 2) // 2)), dma((2, (nz - 2) // 2)),
        ],
        compiler_params=pltpu.CompilerParams(collective_id=0, has_side_effects=True),
    )(old_basis, previous, incoming, coefficient)
    return pl.pallas_call(
        write_out,
        out_shape=(whole, small, small, whole, whole),
        in_specs=[vmem_spec] * 5,
        out_specs=(any_spec,) * 5,
        scratch_shapes=[dma((5,))],
    )(*[pltpu.with_memory_space_constraint(r, pltpu.VMEM) for r in results])


def solution(mesh):
    shape = (mesh.shape["gx"], mesh.shape["gy"], mesh.shape["gz"])
    split = P(None, "gx", "gy", "gz")
    return jax.shard_map(
        functools.partial(per_device, shape), mesh=mesh,
        in_specs=(split, split, split, P("gx", "gy", "gz")),
        out_specs=(split, P(), P(), split, split), check_vma=False,
    )
```

```python
import functools

import jax
import jax.numpy as jnp
from jax import lax
from jax.experimental import pallas as pl
from jax.experimental.pallas import tpu as pltpu
from jax.sharding import PartitionSpec as P

OMEGA = 0.8
HIGH = lax.Precision.HIGHEST
MESH = pl.DeviceIdType.MESH
KS = OMEGA / 6.0
F32 = jnp.float32
ANY = pl.ANY

G0, V0, G1, V1, G2, V2, T2, C1, C0, C2 = range(10)


def iota(shape, dim):
    return lax.broadcasted_iota(jnp.int32, shape, dim)


def roll(x, shift, axis):
    n = x.shape[axis]
    shift = shift % n
    return x if shift == 0 else pltpu.roll(x, shift, axis)


def partner_sum(x, axis, s):
    low = (iota(x.shape, axis) & s) == 0
    return x + jnp.where(low, roll(x, x.shape[axis] - s, axis), roll(x, s, axis))


def coarsen(x, s):
    pairs = x.reshape(*x.shape[:-3], x.shape[-3] // 2, 2, *x.shape[-2:])
    x = pairs[..., 0, :, :] + pairs[..., 1, :, :]
    x = partner_sum(x, x.ndim - 2, s)
    return partner_sum(x, x.ndim - 1, s) * 0.125


def kernel(nx, ny, nz, old_hbm, prev_hbm, inc_hbm, coef_hbm,
           ortho, proj_ref, tri_ref, e0, oper,
           old, prev, inc, coef,
           g0, v0, s0, b1, g1, v1, s1, b2, g2, v2, s2, e2, e1, c1, c2, beyond, h0, h1, h2, exy, ezx, ezy,
           xs, xc, xr, ys, yr, zs, zr, row_s, row_r, line_b, zb, planes, passed, all_planes,
           cc3, inv3, cc4, inv4, inv5, ebuf,
           in_sem, x_send, x_recv, y_send, y_recv, z_send, z_recv,
           d_send, d_recv, ax_send, ax_recv, az_send, az_recv, ag_send, ag_recv):
    gx, gy, gz = lax.axis_index("gx"), lax.axis_index("gy"), lax.axis_index("gz")
    X, Y, Z = 8, 16, 128

    def inside_mesh(place, count):
        return (place >= 0) & (place < count)

    def at(dx=0, dy=0, dz=0):
        return (lax.rem(gx + dx + nx, nx), lax.rem(gy + dy + ny, ny), lax.rem(gz + dz + nz, nz))

    loads = [
        pltpu.make_async_copy(src, dst, in_sem.at[i])
        for i, (src, dst) in enumerate(((coef_hbm, coef), (inc_hbm, inc), (old_hbm, old), (prev_hbm, prev)))
    ]
    for load in loads:
        load.start()

    barrier = pltpu.get_barrier_semaphore()
    for d in range(1, nx):
        pl.semaphore_signal(barrier, inc=1, device_id=at(dx=d), device_id_type=MESH)
    partners = jnp.int32(nx - 1)
    for dz in range(-2, 3):
        reach = (gz + dz >= 0) & (gz + dz < nz)
        partners = partners + jnp.where(reach, ny - (dz == 0), 0)

        @pl.when(reach)
        def _():
            for dy in range(1 if dz == 0 else 0, ny):
                pl.semaphore_signal(barrier, inc=1, device_id=at(dy=dy, dz=dz), device_id_type=MESH)

    lane8, row8 = iota((8, Z), 1), iota((8, Z), 0)
    wide = lambda a: jnp.broadcast_to(a, (8, Z))
    def copy_to(src, dst, ssem, rsem, to):
        return pltpu.make_async_remote_copy(src_ref=src, dst_ref=dst, send_sem=ssem, recv_sem=rsem, device_id=to,
                                            device_id_type=MESH)

    def faces(e, f, n, axis):
        out = []
        for side, d in ((0, 1), (1, -1)):
            if axis == 0:
                if n == 8:
                    src, dst = f.at[:, (n - 1) if side == 0 else 0], xr.at[side, e]
                else:
                    src, dst = xs.at[side, e, pl.ds(0, n)], xc.at[side, e, pl.ds(0, n)]
                copy = copy_to(src, dst, x_send.at[side, e], x_recv.at[side, e], at(dx=d))
                place, count = gx, nx
            elif axis == 1:
                copy = copy_to(ys.at[side, e, :, pl.ds(0, n)], yr.at[side, e, :, pl.ds(0, n)], y_send.at[side, e],
                               y_recv.at[side, e], at(dy=d))
                place, count = gy, ny
            else:
                copy = copy_to(zs.at[side, e], zr.at[side, e], z_send.at[side, e],
                               z_recv.at[side, e], at(dz=d))
                place, count = gz, nz
            out.append((copy, (place + d >= 0) & (place + d < count), (place - d >= 0) & (place - d < count)))
        return out

    sent = []

    def start(e, f, n, axis):
        for copy, sends, _ in faces(e, f, n, axis):
            sent.append((copy, sends))

            @pl.when(sends)
            def _():
                copy.start()

    def send(e, f, n):
        for side, x in ((0, n - 1), (1, 0)):
            for v in range(4):
                if n == 4:
                    xs[side, e, v] = f[v, x, pl.ds(0, 8, stride=2), :]
                elif n == 2:
                    xs[side, e, v // 2, 4 * (v % 2):4 * (v % 2) + 4] = f[v, x, pl.ds(0, 4, stride=4), :]
        start(e, f, n, 0)
        ys[0, e, :, 0:n] = f[:, :, Y - 1:Y, :]
        ys[1, e, :, 0:n] = f[:, :, 0:1, :]
        start(e, f, n, 1)
        packed = [jnp.zeros((8, Z), F32)] * 2
        for i in range(8 * n):
            tile = f[i // (2 * n), i // 2 % n, 8 * (i % 2):8 * (i % 2) + 8]
            here = lane8 == i
            packed = [jnp.where(here, tile[:, x:x + 1], p) for x, p in zip((Z - 1, 0), packed)]
        zs[0, e] = packed[0]
        zs[1, e] = packed[1]
        start(e, f, n, 2)

    def receive(e, f, n):
        for axis in range(3):
            for copy, _, receives in faces(e, f, n, axis):
                @pl.when(receives)
                def _():
                    copy.wait_recv()
        if n < 8:
            for side in range(2):
                for v in range(4):
                    if n == 4:
                        half = xc[side, e, v]
                        for i in range(2):
                            xr[side, e, v, pl.ds(i, 8, stride=2), :] = half
                    else:
                        half = xc[side, e, v // 2, 4 * (v % 2):4 * (v % 2) + 4]
                        for i in range(4):
                            xr[side, e, v, pl.ds(i, 4, stride=4), :] = half

    def edges(level, e, n):
        out = []
        step = (1, -1)
        for kind in range(3):
            for a in range(2):
                for b in range(2):
                    i = 2 * a + b
                    if kind == 0:
                        src, dst = ys.at[b, e, :, pl.ds((n - 1) if a == 0 else 0, 1)], exy.at[level, i]
                        d = dict(dx=step[a], dy=step[b])
                    else:
                        src, dst = zs.at[b, e], (ezx if kind == 1 else ezy).at[level, i]
                        d = {"dx" if kind == 1 else "dy": step[a], "dz": step[b]}
                    full = {"dx": 0, "dy": 0, "dz": 0} | d
                    sends = receives = None
                    for key, place, count in (("dx", gx, nx), ("dy", gy, ny), ("dz", gz, nz)):
                        if full[key]:
                            to, fro = inside_mesh(place + full[key], count), inside_mesh(place - full[key], count)
                            sends = to if sends is None else sends & to
                            receives = fro if receives is None else receives & fro
                    out.append((copy_to(src, dst, d_send.at[kind, level, i], d_recv.at[kind, level, i], at(**d)),
                                sends, receives, dst))
        return out

    def edges_start(level, e, n):
        for copy, sends, _, _ in edges(level, e, n):
            sent.append((copy, sends))

            @pl.when(sends)
            def _():
                copy.start()

    def edges_clear(level, e, n):
        for _, _, receives, dst in edges(level, e, n):
            @pl.when(jnp.logical_not(receives))
            def _():
                dst[...] = jnp.zeros(dst.shape, F32)

    def edges_wait(level, e, n):
        for copy, _, receives, _ in edges(level, e, n):
            @pl.when(receives)
            def _():
                copy.wait_recv()

    def flag(cond):
        return jnp.where(cond, 1.0, 0.0).astype(F32)
    x_in, y_in = (flag(gx > 0), flag(gx < nx - 1)), (flag(gy > 0), flag(gy < ny - 1))
    z_side = (flag(gz > 0), flag(gz < nz - 1))

    def own_part(g, h, n, s):
        per = 8 // n
        for c in range(n // 2):
            part = slice(c * per, (c + 1) * per)
            x = g[part]
            row, lane = iota(x.shape, 2), iota(x.shape, 3)
            near = jnp.where(row >= s, roll(x, s, 2), 0.0) + jnp.where(row < Y - s, roll(x, Y - s, 2), 0.0)
            near = near + jnp.where(lane >= s, roll(x, s, 3), 0.0) + jnp.where(lane < Z - s, roll(x, Z - s, 3), 0.0)
            none = jnp.zeros((per, 1, Y, Z), F32)
            near = near + jnp.concatenate([none, x[:, :-1]], axis=1) + jnp.concatenate([x[:, 1:], none], axis=1)
            h[part] = 1.2 * x + KS * near

    def complete(level, e_g, e, g, n, s):
        edges_wait(level, e_g, n)
        row16, lane16 = iota((Y, Z), 0), iota((Y, Z), 1)
        lane1 = iota((1, Z), 1)
        for side in range(2):
            mine, theirs = (0, n - 1) if side == 0 else (n - 1, 0)
            for v in range(4):
                def column(sz):
                    packed = ezx[level, 2 * side + sz]
                    k = 2 * n * v + 2 * theirs
                    return jnp.concatenate([jnp.broadcast_to(packed[:, k + h:k + h + 1], (8, Z)) for h in range(2)], axis=0)
                add = g[v, mine]
                add = add + jnp.where(row16 < s, exy[level, 2 * side, v, 0], 0.0)
                add = add + jnp.where(row16 >= Y - s, exy[level, 2 * side + 1, v, 0], 0.0)
                add = add + jnp.where(lane16 < s, column(0), 0.0) + jnp.where(lane16 >= Z - s, column(1), 0.0)
                xr[side, e, v] = xr[side, e, v] + (KS * x_in[side]) * add
                for x in range(n):
                    add = g[v, x, 0:1] if side == 0 else g[v, x, Y - 1:Y]
                    for sx, at_x in ((0, 0), (1, n - 1)):
                        if x == at_x:
                            add = add + exy[level, 2 * sx + side, v, 0]
                    k, r = 2 * n * v + 2 * x + (1 if side == 0 else 0), 7 if side == 0 else 0
                    lo, hi = (jnp.broadcast_to(ezy[level, 2 * side + sz, r:r + 1, k:k + 1], (1, Z)) for sz in range(2))
                    add = add + jnp.where(lane1 < s, lo, 0.0) + jnp.where(lane1 >= Z - s, hi, 0.0)
                    yr[side, e, v, x] = yr[side, e, v, x] + (KS * y_in[side]) * add
            add = zs[1 - side, e_g]
            place = lane8 % (2 * n)
            add = add + jnp.where(place < 2, roll(ezx[level, side], -2 * (n - 1), 1), 0.0)
            add = add + jnp.where(place >= 2 * n - 2, roll(ezx[level, 2 + side], 2 * (n - 1), 1), 0.0)
            add = add + jnp.where((row8 < s) & (lane8 % 2 == 0), roll(roll(ezy[level, side], s, 0), -1, 1), 0.0)
            add = add + jnp.where((row8 >= 8 - s) & (lane8 % 2 == 1), roll(roll(ezy[level, 2 + side], -s, 0), 1, 1), 0.0)
            zr[side, e] = zr[side, e] + (KS * z_side[side]) * add

    def z_halo(e, side, first, count):
        packed = zr[side, e]
        return jnp.concatenate([jnp.broadcast_to(packed[:, i:i + 1], (8, Z)) for i in range(first, first + count)], axis=0)

    def along_yz(e, f, n, s, c):
        per = 8 // n
        shape = (per, n, Y, Z)
        x = f[c * per:(c + 1) * per]
        row, lane = iota(shape, 2), iota(shape, 3)
        lo, hi = (yr[side, e, c * per:(c + 1) * per, 0:n] for side in (0, 1))
        total = jnp.where(row >= s, roll(x, s, 2), lo) + jnp.where(row < Y - s, roll(x, Y - s, 2), hi)
        if e == C2:
            out = beyond[c * per:(c + 1) * per]
            return x, (total + jnp.where(lane >= s, roll(x, s, 3), roll(out, s, 3))
                       + jnp.where(lane < Z - s, roll(x, Z - s, 3), roll(out, Z - s, 3)))
        lo, hi = (z_halo(e, side, 16 * c, 16).reshape(shape) for side in (0, 1))
        return x, (total + jnp.where(lane >= s, roll(x, s, 3), lo)
                   + jnp.where(lane < Z - s, roll(x, Z - s, 3), hi))

    def x_ends(e, n, c):
        per = 8 // n
        return (xr[side, e, c * per:(c + 1) * per][:, None] for side in (0, 1))

    def neighbours(e, f, n, s, c):
        x, total = along_yz(e, f, n, s, c)
        lo, hi = x_ends(e, n, c)
        if n > 1:
            lo = jnp.concatenate([lo, x[:, :-1]], axis=1)
            hi = jnp.concatenate([x[:, 1:], hi], axis=1)
        return x, total + lo + hi

    def second_sweep(e, g, v, n, s):
        receive(e, g, n)
        per = 8 // n
        for c in range(n // 2):
            x, near = neighbours(e, g, n, s, c)
            v[c * per:(c + 1) * per] = 1.2 * x + KS * near

    def residual(e, b, c_hat, g, v, third, n, s, put):
        per = 8 // n
        for c in range(n // 2):
            part = slice(c * per, (c + 1) * per)
            x, near = neighbours(e, v, n, s, c)
            third[part] = 0.2 * x + g[part] + KS * near
            put(part, coarsen(b[part] - c_hat * (6.0 * x - near), s))

    def corrected(e, coarse, third, out, n, s):
        per = 8 // n
        for c in range(n // 2):
            part = slice(c * per, (c + 1) * per)
            x, near = along_yz(e, coarse, n, s, c)
            near = near + x
            lo, hi = x_ends(e, n, c)
            if n > 1:
                lo = jnp.concatenate([lo, x[:, :-1]], axis=1)
                hi = jnp.concatenate([x[:, 1:], hi], axis=1)
            both = jnp.stack([0.2 * x + KS * (near + lo), 0.2 * x + KS * (near + hi)], axis=2)
            out[part] = third[part] + both.reshape(per, 2 * n, Y, Z)

    def line_copies(k):
        return [pltpu.make_async_remote_copy(
            src_ref=row_s.at[k], dst_ref=row_r.at[k, gx], send_sem=ax_send.at[k, d - 1], recv_sem=ax_recv.at[k, d - 1],
            device_id=at(dx=d), device_id_type=MESH) for d in range(1, nx)]

    slabs = [(dy, dz) for dz in (0, -1, 1, -2, 2) for dy in range(ny) if dy or dz]

    def deep_copies(k):
        return [(copy_to(line_b.at[k], zb.at[k, 2 - dz, gy], az_send.at[k, i], az_recv.at[k, i], at(dy=dy, dz=dz)),
                 (gz + dz >= 0) & (gz + dz < nz), (gz - dz >= 0) & (gz - dz < nz)) for i, (dy, dz) in enumerate(slabs)]

    def start_line(k, row):
        row_s[k] = row
        row_r[k, gx] = row
        for copy in line_copies(k):
            copy.start()

    def start_deep(k):
        for copy in line_copies(k):
            copy.wait()
        line_b[k] = row_r[k].reshape(nx, Z)
        for copy, sends, _ in deep_copies(k):
            @pl.when(sends)
            def _():
                copy.start()
        zb[k, 2, gy] = line_b[k]

    def finish_deep(k):
        for copy, _, receives in deep_copies(k):
            @pl.when(receives)
            def _():
                copy.wait_recv()

    rounds = (nz - 2) // 2

    def chain_copies(i):
        out = []
        for side, d in ((0, 2), (1, -2)):
            src = planes.at[pl.ds(0 if side == 0 else 3, 2)] if i == 0 else passed.at[side, i - 1]
            copy = copy_to(src, passed.at[side, i], ag_send.at[side, i], ag_recv.at[side, i], at(dz=d))
            near_row = 3 + 2 * i
            if side == 0:
                out.append((copy, (gz + d < nz) & (gz + d - near_row >= 0), gz - near_row >= 0))
            else:
                out.append((copy, (gz + d >= 0) & (gz + d + near_row < nz), gz + near_row < nz))
        return out

    def chain_start(i):
        if i >= rounds:
            return
        for copy, sends, _ in chain_copies(i):
            @pl.when(sends)
            def _():
                copy.start()

    def chain_wait(i):
        if i >= rounds:
            return
        for copy, _, receives in chain_copies(i):
            @pl.when(receives)
            def _():
                copy.wait_recv()

    def chain_next(i):
        chain_wait(i - 1)
        chain_start(i)

    def to_row(blocks):
        q = blocks.shape[0]
        rows = jnp.zeros((8, Z), F32)
        for i in range(q):
            rows = jnp.where(row8 == i, blocks[i], rows)
        pick = (iota((Z, Z), 0) == 8 * (iota((Z, Z), 1) % 16)).astype(F32)
        rows = lax.dot_general(rows, pick, (((1,), (0,)), ((), ())), precision=HIGH, preferred_element_type=F32)
        return jnp.sum(jnp.where(lane8 // 16 == row8, rows, 0.0), axis=0, keepdims=True)

    def spread(k, q):
        shape = (ny, nx, Z)
        group = iota(shape, 2) // 16
        out = jnp.zeros(shape, F32)
        for i in range(5):
            out = jnp.where(group == i, roll(zb[k, i], 16 * (i - q), 2), out)
        return out

    for dx in (-1, 1):
        for dy, dz in ((-1, 0), (1, 0), (0, -1), (0, 1)):
            reach = (inside_mesh(gx + dx, nx)) & inside_mesh(gy + dy, ny) & inside_mesh(gz + dz, nz)
            partners = partners + jnp.where(reach, 1, 0)

            @pl.when(reach)
            def _():
                pl.semaphore_signal(barrier, inc=1, device_id=at(dx=dx, dy=dy, dz=dz), device_id_type=MESH)

    loads[0].wait()
    loads[1].wait()
    c_fine = coef[...]
    scale = KS / c_fine
    for v in range(4):
        g0[v] = inc[v] * scale
    pl.semaphore_wait(barrier, partners)
    send(G0, g0, 8)
    edges_start(0, G0, 8)
    own_part(g0, h0, 8, 1)
    send(V0, h0, 8)
    for level, e, n in ((0, G0, 8), (1, G1, 4), (2, G2, 2)):
        edges_clear(level, e, n)
    for cond, buf, side in ((gx == 0, xr, 0), (gx == nx - 1, xr, 1), (gx == 0, xc, 0), (gx == nx - 1, xc, 1), (gy == 0, yr, 0), (gy == ny - 1, yr, 1),
                            (gz == 0, zr, 0), (gz == nz - 1, zr, 1)):
        @pl.when(cond)
        def _():
            buf[side] = jnp.zeros(buf.shape[1:], F32)
    for side in range(2):
        for i in range((nz - 2) // 2):
            missing = (gz - 3 - 2 * i < 0) if side == 0 else (gz + 3 + 2 * i >= nz)

            @pl.when(missing)
            def _():
                passed[side, i] = jnp.zeros(passed.shape[2:], F32)
    for d in (-2, -1, 1, 2):
        @pl.when((gz + d < 0) | (gz + d >= nz))
        def _():
            zb[:, 2 + d] = jnp.zeros((2,) + zb.shape[2:], F32)

    ebuf[:, 0] = jnp.zeros(ebuf.shape[:1] + ebuf.shape[2:], F32)
    ebuf[:, ny + 1] = jnp.zeros(ebuf.shape[:1] + ebuf.shape[2:], F32)
    ebuf[:, 1:ny + 1, 0:8] = jnp.zeros((8, ny, 8, Z), F32)
    ebuf[:, 1:ny + 1, 8 + nx:] = jnp.zeros((8, ny, 8, Z), F32)

    c1[...] = coarsen(c_fine, 1)
    c2[...] = coarsen(c1[...], 2)
    c3 = coarsen(c2[...], 4)


    loads[2].wait()
    loads[3].wait()
    pairs = [("p", m, j) for m in range(4) for j in range(4)]
    pairs += [("s", i, j) for i in range(4) for j in range(i, 4)]
    pairs += [("c", i, j) for i in range(4) for j in range(i, 4)]
    sums = [None] * len(pairs)
    for x in range(X):
        vo = [old[m, x] for m in range(4)]
        vp = [prev[m, x] for m in range(4)]
        for p, (kind, i, j) in enumerate(pairs):
            a = (vp if kind == "s" else vo)[i]
            b = (vo if kind == "c" else vp)[j]
            ab = a * b
            ab = ab[0:8] + ab[8:16]
            sums[p] = ab if sums[p] is None else sums[p] + ab
    rows = [jnp.sum(a, axis=0, keepdims=True) for a in sums] + [jnp.zeros((4, Z), F32)]
    rows = jnp.sum(jnp.concatenate(rows, axis=0), axis=1, keepdims=True)
    at_lane = iota((40, Z), 1) == iota((40, Z), 0) + 64
    gram_row = jnp.sum(jnp.where(at_lane, rows, 0.0), axis=0, keepdims=True)
    start_line(0, to_row(c3.reshape(2, 8, Z)) + gram_row)

    second_sweep(G0, g0, v0, 8, 1)
    receive(V0, h0, 8)
    complete(0, G0, V0, g0, 8, 1)

    def put_b1(part, r):
        b1[part] = r
        g1[part] = r * scale1
    scale1 = (4.0 * KS) / c1[...]
    residual(V0, inc, c_fine, g0, v0, s0, 8, 1, put_b1)
    send(G1, g1, 4)
    edges_start(1, G1, 4)
    own_part(g1, h1, 4, 2)
    send(V1, h1, 4)
    start_deep(0)

    second_sweep(G1, g1, v1, 4, 2)
    receive(V1, h1, 4)
    complete(1, G1, V1, g1, 4, 2)
    scale2 = (16.0 * KS) / c2[...]

    def put_b2(part, r):
        b2[part] = r
        g2[part] = r * scale2
    residual(V1, b1, 0.25 * c1[...], g1, v1, s1, 4, 2, put_b2)
    send(G2, g2, 2)
    edges_start(2, G2, 2)
    own_part(g2, h2, 2, 4)
    send(V2, h2, 2)
    finish_deep(0)
    for i in range(5):
        planes[i] = jnp.sum(zb[0, i].reshape(ny * nx, Z), axis=0, keepdims=True)
    chain_start(0)
    second_sweep(G2, g2, v2, 2, 4)
    receive(V2, h2, 2)
    complete(2, G2, V2, g2, 2, 4)
    held = []
    residual(V2, b2, 0.0625 * c2[...], g2, v2, s2, 2, 4, lambda part, r: held.append(r))
    start_line(1, to_row(held[0].reshape(8, 8, Z)))
    send(T2, s2, 2)
    chain_next(1)

    shape = (ny, nx, Z)
    lanes = iota(shape, 2)
    place = (gz - 2) * 16 + lanes
    inside = (place >= 0) & (place < nz * 16) & (lanes < 80)
    km = jnp.where(inside, KS, 0.0)
    c3g = [jnp.where(inside, spread(0, q), 1.0) for q in range(2)]
    for q in range(2):
        cc3[q] = (1.0 / 64) * c3g[q]
        inv3[q] = jnp.where(inside, (64.0 * KS) / c3g[q], 0.0)

    def coarsen_gathered(x, s):
        x = partner_sum(x, 1, s)
        return partner_sum(x, 2, s) * 0.125
    c4g = coarsen_gathered(c3g[0] + c3g[1], 1)
    cc4[...] = (1.0 / 256) * c4g
    inv4[...] = jnp.where(inside, (256.0 * KS) / c4g, 0.0)
    halved = c4g.reshape(ny // 2, 2, nx, Z)
    c5g = coarsen_gathered(halved[:, 0] + halved[:, 1], 2)
    inv5[...] = jnp.where(inside[:ny // 2], (1024.0 * KS) / c5g, 0.0)

    start_deep(1)

    chain_next(2)
    finish_deep(1)
    chain_next(3)
    chain_next(4)

    rows_i = iota(shape, 1)
    zero = jnp.zeros((1, nx, Z), F32)

    def along_xz(v, s):
        r = rows_i[:v.shape[0]]
        out = jnp.where(r >= s, roll(v, s, 1), 0.0) + jnp.where(r < nx - s, roll(v, nx - s, 1), 0.0)
        return out + roll(v, s, 2) + roll(v, Z - s, 2)

    def up(v):
        return zero if v.shape[0] == 1 else jnp.concatenate([v[1:], zero], axis=0)

    def down(v):
        return zero if v.shape[0] == 1 else jnp.concatenate([zero, v[:-1]], axis=0)

    def near3(v):
        return [along_xz(v[0], 1) + v[1] + down(v[1]), along_xz(v[1], 1) + v[0] + up(v[0])]

    def near_coarse(v, s):
        return along_xz(v, s) + up(v) + down(v)

    km5 = km[:ny // 2]
    for vec in range(4):
        b = [spread(1, 2 * vec + q) for q in range(2)]
        g = [b[q] * inv3[q] for q in range(2)]
        near = near3(g)
        v = [1.2 * g[q] + km * near[q] for q in range(2)]
        near = near3(v)
        third = [0.2 * v[q] + g[q] + km * near[q] for q in range(2)]
        r = [b[q] - cc3[q] * (6.0 * v[q] - near[q]) for q in range(2)]
        b4 = coarsen_gathered(jnp.where(inside, r[0] + r[1], 0.0), 1)
        g4 = b4 * inv4[...]
        v4 = 1.2 * g4 + km * near_coarse(g4, 2)
        n4 = near_coarse(v4, 2)
        third4 = 0.2 * v4 + g4 + km * n4
        r4_ = b4 - cc4[...] * (6.0 * v4 - n4)
        r4_ = jnp.where(inside, r4_, 0.0).reshape(ny // 2, 2, nx, Z)
        g5 = coarsen_gathered(r4_[:, 0] + r4_[:, 1], 2) * inv5[...]
        v5 = g5
        for _ in range(3):
            v5 = 0.2 * v5 + g5 + km5 * near_coarse(v5, 4)
        p4 = jnp.stack([v5, v5], axis=1).reshape(ny, nx, Z)
        e4 = third4 + 0.2 * p4 + km * near_coarse(p4, 2)
        xz = along_xz(e4, 1)
        ebuf[2 * vec, 1:ny + 1, 8:8 + nx] = third[0] + 0.2 * e4 + km * (xz + e4 + down(e4))
        ebuf[2 * vec + 1, 1:ny + 1, 8:8 + nx] = third[1] + 0.2 * e4 + km * (xz + e4 + up(e4))

    receive(T2, s2, 2)
    around = [(dx, dy) for dx in (-1, 0, 1) for dy in (0, -1, 1)]
    stacked = jnp.concatenate([ebuf[:, gy + 1 + dy, pl.ds(8 + gx + dx, 1), :].reshape(8, Z) for dx, dy in around], axis=0)
    li, lj = iota((Z, Z), 0), iota((Z, Z), 1)
    after = lj < 64
    maps = [li == 32 + lj // 8, (li == 31 + (lj + 4) // 8) | (li == 32 + (lj + 4) // 8),
            li == jnp.where(after, 48, 31), (li == jnp.where(after, 47, 31)) | (li == jnp.where(after, 48, 32))]
    spread_rows = [lax.dot_general(stacked, m.astype(F32), (((1,), (0,)), ((), ())), precision=HIGH,
                                   preferred_element_type=F32) for m in maps]

    def cell(kind, vec, y2, dx, dy=0):
        i = 8 * around.index((dx, dy)) + 2 * vec + y2
        return wide(spread_rows[kind][i:i + 1])

    z_in = jnp.where(lane8 < 64, flag(gz < nz - 1), flag(gz > 0))
    third_out = jnp.where(iota((128, Z), 1) < 64, z_halo(T2, 1, 0, 16), z_halo(T2, 0, 0, 16)).reshape(4, 2, Y, Z)
    for vec in range(4):
        for dx, others in ((0, (-1, 1)), (-1, (0,)), (1, (0,))):
            for kind in (0, 2) if dx == 0 else (0,):
                a = [cell(kind, vec, y2, dx) for y2 in range(2)]
                mid = a[0] + a[1]
                y_sum = [jnp.where(row8 < 4, cell(kind, vec, 1, dx, -1) + a[0], mid),
                         jnp.where(row8 < 4, mid, a[1] + cell(kind, vec, 0, dx, 1))]
                for h in range(2):
                    part = slice(8 * h, 8 * h + 8)
                    base = 0.2 * a[h] + KS * (y_sum[h] + cell(kind + 1, vec, h, dx) + a[h])
                    for x, other in enumerate(others):
                        value = base + KS * cell(kind, vec, h, other)
                        if dx:
                            side = 0 if dx < 0 else 1
                            xr[side, C2, vec, part] = xr[side, T2, vec, part] + x_in[side] * value
                        elif kind == 0:
                            e2[vec, x, part] = s2[vec, x, part] + value
                        else:
                            beyond[vec, x, part] = third_out[vec, x, part] + z_in * value
        for side, dy, y2 in ((0, -1, 1), (1, 1, 0)):
            b = cell(0, vec, y2, 0, dy)[0:1]
            base = 0.2 * b + KS * (2.0 * b + cell(0, vec, 1 - y2, 0)[0:1] + cell(1, vec, y2, 0, dy)[0:1])
            for x, dx in enumerate((-1, 1)):
                value = base + KS * cell(0, vec, y2, dx, dy)[0:1]
                yr[side, C2, vec, x] = yr[side, T2, vec, x] + y_in[side] * value

    corrected(C2, e2, s1, e1, 2, 2)
    send(C1, e1, 4)
    chain_next(5)
    receive(C1, e1, 4)
    chain_next(6)
    corrected(C1, e1, s0, e0, 4, 1)
    send(C0, e0, 8)
    for i in range(7, rounds + 1):
        chain_next(i)
    for i in range(5):
        all_planes[gz + nz + i - 2] = planes[i]
    for i in range(rounds):
        for j in range(2):
            all_planes[gz + nz - 4 - 2 * i + j] = passed[0, i, j]
            all_planes[gz + nz + 3 + 2 * i + j] = passed[1, i, j]
    line = jnp.sum(all_planes[nz:2 * nz].reshape(nz, Z), axis=0, keepdims=True)
    column = jnp.sum(jnp.where(at_lane, line, 0.0), axis=1, keepdims=True)
    column = column * (1.0 / float(nx * ny * nz * X * Y * Z))
    value = {key: column[p:p + 1] for p, key in enumerate(pairs)}
    for kind in "sc":
        for i in range(4):
            for j in range(i):
                value[kind, i, j] = value[kind, j, i]
    proj = [[value["p", m, j] for j in range(4)] for m in range(4)]
    mixed = [[sum(value["c", m, n] * proj[n][j] for n in range(4)) for j in range(4)] for m in range(4)]
    low = [[None] * 4 for _ in range(4)]
    inverse = [[None] * 4 for _ in range(4)]
    for j in range(4):
        for i in range(j, 4):
            g = value["s", i, j] + sum(proj[m][i] * (mixed[m][j] - 2.0 * proj[m][j]) for m in range(4))
            for k in range(j):
                g = g - low[i][k] * low[j][k]
            low[i][j] = jnp.sqrt(g) if i == j else g / low[j][j]
    for j in range(4):
        inverse[j][j] = 1.0 / low[j][j]
        for i in range(j + 1, 4):
            inverse[i][j] = -sum(low[i][k] * inverse[k][j] for k in range(j, i)) * (1.0 / low[i][i])
    r4, l4 = iota((4, 4), 0), iota((4, 4), 1)
    out_p, out_t = jnp.zeros((4, 4), F32), jnp.zeros((4, 4), F32)
    for i in range(4):
        for j in range(4):
            here = (r4 == i) & (l4 == j)
            out_p = jnp.where(here, proj[i][j], out_p)
            if j >= i:
                out_t = jnp.where(here, low[j][i], out_t)
    proj_ref[...] = out_p
    tri_ref[...] = out_t
    proj_w = [[wide(a) for a in line_] for line_ in proj]
    inv_w = [[wide(inverse[j][i]) if i <= j else None for i in range(4)] for j in range(4)]
    for x in range(X):
        for h in range(2):
            part = slice(8 * h, 8 * h + 8)
            vo = [old[m, x, part] for m in range(4)]
            rem = [prev[j, x, part] - sum(proj_w[m][j] * vo[m] for m in range(4)) for j in range(4)]
            for j in range(4):
                ortho[j, x, part] = sum(inv_w[j][i] * rem[i] for i in range(j + 1))

    for i in range(rounds):
        sent[:0] = [(copy, sends) for copy, sends, _ in chain_copies(i)]
    for k in range(2):
        sent[:0] = [(copy, sends) for copy, sends, _ in deep_copies(k)]
    for copy, sends in sent[:-6]:
        @pl.when(sends)
        def _():
            copy.wait_send()
    receive(C0, e0, 8)
    for c in range(4):
        x, near = neighbours(C0, e0, 8, 1, c)
        oper[c:c + 1] = c_fine * (6.0 * x - near)
    for copy, sends in sent[-6:]:
        @pl.when(sends)
        def _():
            copy.wait_send()


def write_out(*refs):
    sems = refs[-1]
    copies = [pltpu.make_async_copy(refs[i], refs[5 + i], sems.at[i]) for i in range(5)]
    for copy in copies:
        copy.start()
    for copy in copies:
        copy.wait()


def per_device(shape, old_basis, previous, incoming, coefficient):
    nx, ny, nz = shape
    big = pltpu.VMEM((4, 8, 16, 128), F32)
    mid = pltpu.VMEM((4, 4, 16, 128), F32)
    low = pltpu.VMEM((4, 2, 16, 128), F32)
    dma = pltpu.SemaphoreType.DMA
    vm = lambda *s: pltpu.VMEM(s, F32)
    whole = jax.ShapeDtypeStruct((4, 8, 16, 128), F32)
    small = jax.ShapeDtypeStruct((4, 4), F32)
    held = (vm(4, 8, 16, 128), vm(4, 4), vm(4, 4), vm(4, 8, 16, 128), vm(4, 8, 16, 128))
    any_spec = pl.BlockSpec(memory_space=pl.ANY)
    vmem_spec = pl.BlockSpec(memory_space=pltpu.VMEM)
    results = pl.pallas_call(
        functools.partial(kernel, nx, ny, nz),
        out_shape=held,
        in_specs=[any_spec] * 4,
        out_specs=(vmem_spec,) * 5,
        scratch_shapes=[
            big, big, big, vm(8, 16, 128),
            big, big, big, mid, mid, mid, mid, low, low, low, low, low, mid, vm(4, 16, 128), vm(2, 16, 128), low,
            big, mid, low, vm(3, 4, 4, 1, 1, 128), vm(3, 4, 8, 128), vm(3, 4, 8, 128),
            vm(2, 9, 4, 8, 128), vm(2, 9, 4, 8, 128), vm(2, 10, 4, 16, 128), vm(2, 9, 4, 8, 1, 128),
            vm(2, 10, 4, 8, 1, 128), vm(2, 9, 8, 128), vm(2, 9, 8, 128),
            vm(2, 1, 128), vm(2, nx, 1, 128), vm(2, nx, 128), vm(2, 5, ny, nx, 128), vm(5, 1, 128), vm(2, (nz - 2) // 2, 2, 1, 128), vm(3 * nz, 1, 128),
            vm(2, ny, nx, 128), vm(2, ny, nx, 128), vm(ny, nx, 128), vm(ny, nx, 128), vm(ny // 2, nx, 128),
            vm(8, ny + 2, nx + 16, 128),
            dma((4,)), dma((2, 9)), dma((2, 9)), dma((2, 9)), dma((2, 9)), dma((2, 9)), dma((2, 9)),
            dma((3, 3, 4)), dma((3, 3, 4)), dma((2, nx - 1)), dma((2, nx - 1)), dma((2, 5 * ny - 1)), dma((2, 5 * ny - 1)),
            dma((2, (nz - 2) // 2)), dma((2, (nz - 2) // 2)),
        ],
        compiler_params=pltpu.CompilerParams(collective_id=0, has_side_effects=True),
    )(old_basis, previous, incoming, coefficient)
    return pl.pallas_call(
        write_out,
        out_shape=(whole, small, small, whole, whole),
        in_specs=[vmem_spec] * 5,
        out_specs=(any_spec,) * 5,
        scratch_shapes=[dma((5,))],
    )(*[pltpu.with_memory_space_constraint(r, pltpu.VMEM) for r in results])


def solution(mesh):
    shape = (mesh.shape["gx"], mesh.shape["gy"], mesh.shape["gz"])
    split = P(None, "gx", "gy", "gz")
    return jax.shard_map(
        functools.partial(per_device, shape), mesh=mesh,
        in_specs=(split, split, split, P("gx", "gy", "gz")),
        out_specs=(split, P(), P(), split, split), check_vma=False,
    )
```
